32 devices in a mesh: dp: 8 (over y, x, core), space: 4 (over z).
Axes of the slice: x: 2, y: 2, z: 4, core: 2. Of those that a mesh axis runs over, the one named last changes fastest.
Arguments:
- inputs: bfloat16 [64, 32, 32, 1024], P('dp', None, 'space'), may hold values from 0 to 2
- conv_in: bfloat16 [64, 864], replicated, may hold values from -0.21875 to 0.21875
- norm_gain: float32 [64], replicated, may hold values from 0.5 to 1.5
- norm_shift: float32 [64], replicated, may hold values from -3 to 3
- conv_out: bfloat16 [128, 1728], replicated, may hold values from -0.15625 to 0.15625
- dense_in: bfloat16 [65536, 128], replicated, may hold values from -0.0234375 to 0.0234375
- dense_out: bfloat16 [128, 4], replicated, may hold values from -0.5 to 0.5
- targets: float32 [64, 4], P(('dp', 'space')), may hold values from -6 to 6
Outputs:
- grad_conv_in: float32 [64, 864], replicated
- grad_norm: float32 [2, 64], replicated
- grad_conv_out: float32 [128, 1728], replicated
- grad_dense_in: float32 [65536, 128], P(('dp', 'space'))
- grad_dense_out: float32 [128, 4], replicated
- predictions: float32 [64, 4], P(('dp', 'space'))
The draws below stay inside these ranges and needn't reach their ends.
All inputs are finite; a program needn't handle non-finite values.
Results may differ from the reference program's by a relative error of at most 0.015.
Values may be sent and summed in bfloat16 or wider, within the bound.
No kernel may reach another device: no remote copies, remote signals or barrier semaphores. Data moves between devices by JAX's collectives and lax.ppermute only.
A program may use at most 256 MiB of HBM per device.

```python
import jax
import jax.numpy as jnp
from jax import lax

C_IN = 32
C_MID = 64
C_OUT = 128
DENSE = 128
TARGETS = 4
GRID = 32
B_DEV = 8
BATCH = 64
FLAT = 65536
N_DP = 8


def levels(key, extent, split, low, top_value):
    gain, own = 1.0, jax.random.fold_in(key, 6)
    for axis_at, parts in split:
        draws = jnp.exp(jax.random.uniform(jax.random.fold_in(own, axis_at), (parts,), jnp.float32, low / len(split), top_value / len(split)))
        gain = gain * jnp.repeat(draws, extent[axis_at] // parts).reshape([-1 if axis == axis_at else 1 for axis in range(len(extent))])
    return gain


def bell_draw(stream_key, dims, scale, limit, cuts=(), kind=jnp.bfloat16):
    gain = levels(stream_key, dims, cuts, -0.22, 0.18) if cuts else 1.0
    array = jax.random.normal(stream_key, dims, jnp.float32) * scale * gain
    return jnp.minimum(jnp.maximum(array, -limit), limit).astype(kind)


def setup_inputs(seed: int = 0) -> dict:
    seeds = jax.random.split(jax.random.key(seed), 9)
    return {
        "inputs": jnp.clip(2.0 * jax.random.uniform(seeds[0], (BATCH, C_IN, GRID, GRID * GRID), jnp.float32) ** levels(seeds[0], (BATCH, C_IN, GRID, GRID * GRID), ((0, 8), (2, 4)), -0.2, 0.2), 0.0, 2.0).astype(jnp.bfloat16),
        "conv_in": bell_draw(seeds[1], (C_MID, 27 * C_IN), (27 * C_IN) ** -0.5, 0.21875),
        "norm_gain": jnp.clip(1.0 + 0.1 * jax.random.normal(seeds[2], (C_MID,), jnp.float32), 0.5, 1.5),
        "norm_shift": bell_draw(seeds[3], (C_MID,), 0.5, 3.0, (), jnp.float32),
        "conv_out": bell_draw(seeds[4], (C_OUT, 27 * C_MID), (27 * C_MID) ** -0.5, 0.15625),
        "dense_in": bell_draw(seeds[5], (FLAT, DENSE), FLAT ** -0.5, 0.0234375),
        "dense_out": bell_draw(seeds[6], (DENSE, TARGETS), DENSE ** -0.5, 0.5),
        "targets": bell_draw(seeds[7], (BATCH, TARGETS), 1.0, 6.0, ((0, 32),), jnp.float32),
    }


norm_epsilon = 1e-05

def leaky_relu(values):
    return 0.65 * values + 0.35 * values * jnp.tanh(values)

def slope_of(values):
    bent = jnp.tanh(values)
    return 0.65 + 0.35 * (bent + values * (1.0 - bent * bent))

def unfold_volume(volume):
    channels, size_x, size_y, size_z = volume.shape
    padded = jnp.pad(volume, ((0, 0), (1, 1), (1, 1), (1, 1)))
    pieces = []
    for step_x in (-1, 0, 1):
        for step_y in (-1, 0, 1):
            for step_z in (-1, 0, 1):
                window = padded[:, 1 + step_x:1 + step_x + size_x, 1 + step_y:1 + step_y + size_y, 1 + step_z:1 + step_z + size_z]
                pieces.append(window.reshape(channels, size_x * size_y * size_z))
    return jnp.concatenate(pieces, axis=0)

def pool_volume(volume):
    leading = volume.shape[:-3]
    size_x, size_y, size_z = volume.shape[-3:]
    blocks = volume.reshape(leading + (size_x // 2, 2, size_y // 2, 2, size_z // 2, 2))
    return blocks.sum(axis=(-5, -3, -1)) * 0.125

def spread_grad(gradient):
    leading = gradient.shape[:-3]
    size_x, size_y, size_z = gradient.shape[-3:]
    blocks = gradient.reshape(leading + (size_x, 1, size_y, 1, size_z, 1))
    wide = jnp.broadcast_to(blocks, leading + (size_x, 2, size_y, 2, size_z, 2))
    return wide.reshape(leading + (2 * size_x, 2 * size_y, 2 * size_z)) * 0.125

def reference(inputs, conv_in, norm_gain, norm_shift, conv_out, dense_in, dense_out, targets):
    half_grid = GRID // 2
    quarter = GRID // 4
    cell_total = GRID ** 3
    cell_count = B_DEV * cell_total
    volumes = inputs.reshape(BATCH, C_IN, GRID, GRID, GRID)
    first_out = lax.map(lambda volume: jnp.dot(conv_in, unfold_volume(volume), preferred_element_type=jnp.float32), volumes)
    grouped = first_out.reshape(N_DP, B_DEV, C_MID, cell_total)
    average = lax.optimization_barrier(jnp.sum(grouped, axis=(1, 3), keepdims=True)) / cell_count
    centred = grouped - average
    variance = lax.optimization_barrier(jnp.sum(centred * centred, axis=(1, 3), keepdims=True)) / cell_count
    inverse = lax.rsqrt(variance + norm_epsilon)
    whitened = centred * inverse
    scale_row = norm_gain[None, None, :, None]
    normed = scale_row * whitened + norm_shift[None, None, :, None]
    pooled = pool_volume(leaky_relu(normed).reshape(BATCH, C_MID, GRID, GRID, GRID)).astype(jnp.bfloat16)
    second_out = lax.map(lambda volume: jnp.dot(conv_out, unfold_volume(volume), preferred_element_type=jnp.float32), pooled)
    features = pool_volume(leaky_relu(second_out).reshape(BATCH, C_OUT, half_grid, half_grid, half_grid))
    features = features.reshape(BATCH, FLAT).astype(jnp.bfloat16)
    hidden_pre = jnp.dot(features, dense_in, preferred_element_type=jnp.float32)
    hidden = leaky_relu(hidden_pre).astype(jnp.bfloat16)
    predictions = jnp.dot(hidden, dense_out, preferred_element_type=jnp.float32)
    misfit = predictions - targets
    grad_dense_out = jnp.dot(hidden.astype(jnp.float32).T, misfit, precision=lax.Precision.HIGHEST)
    back_hidden = (jnp.dot(misfit, dense_out.astype(jnp.float32).T, precision=lax.Precision.HIGHEST) * slope_of(hidden_pre)).astype(jnp.bfloat16)
    grad_dense_in = jnp.dot(features.T, back_hidden, preferred_element_type=jnp.float32)
    back_features = jnp.dot(back_hidden, dense_in.T, preferred_element_type=jnp.float32)
    back_features = back_features.reshape(BATCH, C_OUT, quarter, quarter, quarter)
    back_second = (spread_grad(back_features).reshape(BATCH, C_OUT, half_grid ** 3) * slope_of(second_out)).astype(jnp.bfloat16)

    def second_back(running, couple):
        volume, gradient = couple
        patches = unfold_volume(volume)
        running = running + jnp.dot(gradient, patches.T, preferred_element_type=jnp.float32)
        patch_grad = jnp.dot(conv_out.T, gradient, preferred_element_type=jnp.float32)
        _, unfold = jax.vjp(unfold_volume, volume.astype(jnp.float32))
        return (running, unfold(patch_grad)[0].astype(jnp.bfloat16))
    grad_conv_out, back_pooled = lax.scan(second_back, jnp.zeros((C_OUT, 27 * C_MID), jnp.float32), (pooled, back_second))
    back_active = spread_grad(back_pooled.astype(jnp.float32)).reshape(N_DP, B_DEV, C_MID, cell_total) * slope_of(normed)
    sum_grad = lax.optimization_barrier(jnp.sum(back_active, axis=(1, 3), keepdims=True))
    sum_xgrad = lax.optimization_barrier(jnp.sum(back_active * whitened, axis=(1, 3), keepdims=True))
    grad_norm = jnp.stack([lax.optimization_barrier(jnp.sum(sum_xgrad, axis=(0, 1, 3))), lax.optimization_barrier(jnp.sum(sum_grad, axis=(0, 1, 3)))])
    back_first = scale_row * inverse * (back_active - sum_grad / cell_count - whitened * sum_xgrad / cell_count)
    back_first = back_first.astype(jnp.bfloat16).reshape(BATCH, C_MID, cell_total)

    def first_back(running, couple):
        volume, gradient = couple
        return (running + jnp.dot(gradient, unfold_volume(volume).T, preferred_element_type=jnp.float32), None)
    grad_conv_in, _ = lax.scan(first_back, jnp.zeros((C_MID, 27 * C_IN), jnp.float32), (volumes, back_first))
    return (grad_conv_in, grad_norm, grad_conv_out, grad_dense_in, grad_dense_out, predictions)
```

```python
import jax
import jax.numpy as jnp
import numpy as np
from jax import lax
from jax.experimental import pallas as pl
from jax.experimental.pallas import tpu as pltpu
from jax.sharding import PartitionSpec as P

GRID = 32
HALVES = 2
LANES = 128
norm_epsilon = 1e-05
INTERPRET = False

F32 = jnp.float32
BF16 = jnp.bfloat16


def leaky_relu(values):
    return values * (0.65 + 0.35 * jnp.tanh(values))


def slope_of(values):
    bent = jnp.tanh(values)
    return 0.65 + 0.35 * (bent + values * (1.0 - bent * bent))


def dot(a, b):
    return jnp.dot(a, b, preferred_element_type=F32)


def dot_rows(a, b):
    return lax.dot_general(a, b, (((0,), (0,)), ((), ())), preferred_element_type=F32)


def dot_lanes(a, b):
    return lax.dot_general(a, b, (((1,), (1,)), ((), ())), preferred_element_type=F32)


def low_half(shape):
    return lax.broadcasted_iota(jnp.int32, shape, len(shape) - 1) < LANES // 2


def roll_half(values):
    flat = values.reshape(-1, LANES)
    return pltpu.roll(flat, LANES // 2, 1).reshape(values.shape)


def both_halves(values):
    return values + roll_half(values)


def call(kernel, out_shape, **kwargs):
    return pl.pallas_call(kernel, out_shape=out_shape, interpret=INTERPRET, **kwargs)


def whole_spec(shape):
    return pl.BlockSpec(shape, lambda *_: (0,) * len(shape), pipeline_mode=pl.Buffered(1))


def first_weights(conv_in):
    co = conv_in.shape[0]
    c = conv_in.shape[1] // 27
    w = conv_in.reshape(co, 3, 3, 3, c).transpose(3, 1, 2, 4, 0)
    parts = [
        jnp.pad(w, ((0, 0), (px, 1 - px), (py, 1 - py), (0, 0), (0, 0)))
        for px in (0, 1)
        for py in (0, 1)
    ]
    w = jnp.stack(parts, axis=4).reshape(3, 2, 2, 2, 2, c, 4 * co)
    return w.transpose(0, 1, 3, 4, 2, 5, 6).reshape(3 * 16 * c, 4 * co)


def second_weights(conv_out):
    co = conv_out.shape[0]
    c = conv_out.shape[1] // 27
    w = conv_out.reshape(co, 3, 3, 3, c).transpose(2, 3, 1, 4, 0)
    parts = [jnp.pad(w, ((0, 0), (0, 0), (px, 1 - px), (0, 0), (0, 0))) for px in (0, 1)]
    return jnp.stack(parts, axis=4).reshape(9 * 4 * c, 2 * co)


def adjoint_weights(conv_out):
    co = conv_out.shape[0]
    c = conv_out.shape[1] // 27
    w = conv_out.reshape(co, 3, 3, 3, c)[:, ::-1, ::-1, ::-1].transpose(3, 1, 2, 0, 4)
    parts = [
        jnp.pad(w, ((0, 0), (px, 1 - px), (py, 1 - py), (0, 0), (0, 0)))
        for px in (0, 1)
        for py in (0, 1)
    ]
    return jnp.stack(parts, axis=4).reshape(48 * co, 4 * c)


def half_pads(before, after):
    zero = jnp.zeros_like(before[:, 0:8])
    return (
        jnp.concatenate([zero, before[:, 0:8]], axis=1),
        jnp.concatenate([after[:, 8:16], zero], axis=1),
    )


def first_kernel(planes, samples, refs):
    (x_ref, halo_ref, pa_ref, pb_ref, w_ref, f_ref, xb_ref, st_ref, z_ref, w_acc) = refs
    i = pl.program_id(0)
    pairs = planes // 2 + 1
    half_y = GRID // HALVES
    chunks = z_ref.shape[0]
    inner = HALVES * samples
    groups = GRID * GRID // LANES
    per_group = LANES // GRID

    @pl.when(i == 0)
    def _():
        def gather(t, carry):
            s = t % samples
            q = t // samples
            for h in range(HALVES):
                g = q + h * (groups // HALVES)
                lanes = pl.ds(pl.multiple_of(g * LANES, LANES), LANES)
                t_val = dot_rows(x_ref[s, :, lanes], pa_ref[...]) + dot_rows(
                    halo_ref[s, :, lanes], pb_ref[...]
                )
                start = (per_group * q + 1) * GRID * inner + h * samples + s
                for k in range(chunks):
                    z_ref[k, pl.ds(start, LANES, stride=inner), :] = t_val[
                        :, k * LANES : (k + 1) * LANES
                    ]
            return carry

        lax.fori_loop(0, samples * groups // HALVES, gather, 0)
        row = GRID * inner

        def plane_of(k, y):
            start = pl.multiple_of(y * row, row)
            return z_ref[k, pl.ds(start, row), :]

        for k in range(chunks):
            last = plane_of(k, half_y).reshape(GRID, inner, LANES)
            head = plane_of(k, 1).reshape(GRID, inner, LANES)
            lo, hi = half_pads(last, head)
            z_ref[k, 0:row, :] = lo.reshape(row, LANES)
            z_ref[k, (half_y + 1) * row : (half_y + 2) * row, :] = hi.reshape(row, LANES)

        def assemble(m, carry):
            mask = low_half((row, LANES))
            for k in range(pairs):
                a = plane_of(k // 2, 2 * m)
                b = plane_of(k // 2, 2 * m + 1)
                if k % 2 == 0:
                    b = roll_half(b)
                else:
                    a = roll_half(a)
                both = jnp.where(mask, a, b).astype(BF16)
                xb_ref[k, m, 1 : GRID + 1] = both.reshape(GRID, inner, LANES)
                zero = jnp.zeros((inner, LANES), BF16)
                xb_ref[k, m, 0] = zero
                xb_ref[k, m, GRID + 1] = zero
            return carry

        lax.fori_loop(0, half_y // 2 + 1, assemble, 0)
        w_acc[...] = jnp.zeros_like(w_acc)

    rows = GRID * inner
    blocks = half_y // 2
    per_block = rows // 8

    def conv(yb, carry):
        pieces = []
        for dz in range(3):
            for kk in range(2):
                for mm in range(2):
                    pieces.append(
                        xb_ref[i + kk, yb + mm, dz : dz + GRID].reshape(rows, LANES)
                    )
        out = dot(jnp.concatenate(pieces, axis=1), w_ref[...])
        f_ref[0, yb] = out.reshape(GRID, inner, 2 * LANES)
        stacked = out.reshape(per_block, 8, 2 * LANES)
        mean = jnp.sum(stacked, axis=0) * (1.0 / per_block)
        dev = stacked - mean[None]
        square = jnp.sum(dev * dev, axis=0)
        done = (i * blocks + yb).astype(F32)
        delta = mean - w_acc[0]
        w_acc[0] = w_acc[0] + delta / (done + 1.0)
        w_acc[1] = w_acc[1] + square + delta * delta * (per_block * done / (done + 1.0))
        return carry

    lax.fori_loop(0, blocks, conv, 0)

    @pl.when(i == pl.num_programs(0) - 1)
    def _():
        count = float(per_block * blocks * (planes // 2))
        mean = w_acc[0]
        m = jnp.mean(mean, axis=0, keepdims=True)
        m = both_halves((m[:, :LANES] + m[:, LANES:]) * 0.5) * 0.5
        wide = jnp.concatenate([m, m], axis=1)
        dev = mean - wide
        q = jnp.sum(w_acc[1] + count * dev * dev, axis=0, keepdims=True)
        q = both_halves(q[:, :LANES] + q[:, LANES:])
        st_ref[...] = jnp.concatenate([m, q], axis=0)


def first_conv(x, halo, w1, planes):
    samples = x.shape[0]
    c = halo.shape[1] // 2
    pairs = planes // 2 + 1
    used = pairs * 2 * c
    chunks = -(-used // LANES)
    inner = HALVES * samples
    half_y = GRID // HALVES
    pa = np.zeros((c * planes, chunks * LANES), np.float32)
    pb = np.zeros((2 * c, chunks * LANES), np.float32)
    for ch in range(c):
        for p in range(planes):
            pa[ch * planes + p, (p + 1) * c + ch] = 1.0
        pb[ch, ch] = 1.0
        pb[c + ch, (planes + 1) * c + ch] = 1.0
    pa = jnp.asarray(pa, BF16)
    pb = jnp.asarray(pb, BF16)
    nxb = planes // 2
    nyb = half_y // 2
    f_shape = (nxb, nyb, GRID, inner, 2 * LANES)
    xb_shape = (pairs, nyb + 1, GRID + 2, inner, LANES)
    return call(
        lambda *refs: first_kernel(planes, samples, refs),
        (
            jax.ShapeDtypeStruct(f_shape, F32),
            jax.ShapeDtypeStruct(xb_shape, BF16),
            jax.ShapeDtypeStruct((2, LANES), F32),
        ),
        grid=(nxb,),
        in_specs=[whole_spec(a.shape) for a in (x, halo, pa, pb, w1)],
        out_specs=(
            pl.BlockSpec((1,) + f_shape[1:], lambda i: (i, 0, 0, 0, 0)),
            whole_spec(xb_shape),
            whole_spec((2, LANES)),
        ),
        scratch_shapes=[
            pltpu.VMEM((chunks, (half_y + 2) * GRID * inner, LANES), F32),
            pltpu.VMEM((2, 8, 2 * LANES), F32),
        ],
        name="first_conv",
    )(x, halo, pa, pb, w1)


def group_stats(st, local_count, total_count):
    means = st[:, 0]
    mean = jnp.mean(means, axis=0, keepdims=True)
    dev = means - mean
    square = jnp.sum(st[:, 1] + local_count * dev * dev, axis=0, keepdims=True)
    inverse = lax.rsqrt(square / total_count + norm_epsilon)
    return mean, inverse


def wide(row):
    return jnp.concatenate([row, row], axis=1)


def pool_kernel(local_count, total_count, f_ref, st_ref, gs_ref, pd_ref, lo_ref, hi_ref):
    i = pl.program_id(0)
    mean, inverse = group_stats(st_ref[...], local_count, total_count)
    mean = wide(mean)
    inverse = wide(inverse)
    gain = wide(gs_ref[0:1])
    shift = wide(gs_ref[1:2])
    nyb = f_ref.shape[1]
    nz = f_ref.shape[2]
    inner = f_ref.shape[3]

    def step(yb, carry):
        f = f_ref[0, yb].reshape(nz * inner, 2 * LANES)
        act = leaky_relu(gain * ((f - mean) * inverse) + shift)
        act = act[:, :LANES] + act[:, LANES:]
        act = act.reshape(nz // 2, 2, inner, LANES)
        act = act[:, 0] + act[:, 1]
        pooled = both_halves(act) * 0.125
        pd_ref[0, yb] = pooled.astype(BF16)
        return carry

    lax.fori_loop(0, nyb, step, 0)
    half = nyb // 2

    def pack(ref):
        mask = low_half((nz // 2, inner, LANES))
        for y in range(half):
            ref[y] = jnp.where(mask, pd_ref[0, y].astype(F32), pd_ref[0, y + half].astype(F32)).astype(BF16)

    @pl.when(i == 0)
    def _():
        pack(lo_ref)

    @pl.when(i == pl.num_programs(0) - 1)
    def _():
        pack(hi_ref)


def normalise_pool(f, st, gs, local_count, total_count):
    nxb, nyb, nz, inner, _ = f.shape
    pd_shape = (nxb, nyb, nz // 2, inner, LANES)
    edge = (nyb // 2, nz // 2, inner, LANES)
    return call(
        lambda *refs: pool_kernel(local_count, total_count, *refs),
        (
            jax.ShapeDtypeStruct(pd_shape, BF16),
            jax.ShapeDtypeStruct(edge, BF16),
            jax.ShapeDtypeStruct(edge, BF16),
        ),
        grid=(nxb,),
        in_specs=[
            pl.BlockSpec((1,) + f.shape[1:], lambda i: (i, 0, 0, 0, 0)),
            whole_spec(st.shape),
            whole_spec(gs.shape),
        ],
        out_specs=(
            pl.BlockSpec((1,) + pd_shape[1:], lambda i: (i, 0, 0, 0, 0)),
            whole_spec(edge),
            whole_spec(edge),
        ),
        name="normalise_pool",
    )(f, st, gs)


def second_kernel(samples, j_ref, pd_ref, lo_ref, hi_ref, w_ref, d_ref, pp_ref, sec_ref, fc_ref, hid_ref, ft, fcs):
    planes, ny, nz, inner, _ = pd_ref.shape
    pairs = planes // 2 + 1
    half = ny // 2
    cells = fc_ref.shape[2]
    channels = fc_ref.shape[0]

    def unpack(ref, y):
        v = ref[y % half].astype(F32)
        return jnp.where(low_half(v.shape) == (y < half), v, roll_half(v))

    def assemble(y, carry):
        mask = low_half((nz, inner, LANES))
        for k in range(pairs):
            a = unpack(lo_ref, y) if k == 0 else pd_ref[2 * k - 1, y].astype(F32)
            b = unpack(hi_ref, y) if k == pairs - 1 else pd_ref[2 * k, y].astype(F32)
            pp_ref[k, y + 1, 1 : nz + 1] = jnp.where(mask, a, b).astype(BF16)
        return carry

    lax.fori_loop(0, ny, assemble, 0)
    zero = jnp.zeros((inner, LANES), BF16)
    for k in range(pairs):
        last = pp_ref[k, ny, 1 : nz + 1].astype(F32)
        head = pp_ref[k, 1, 1 : nz + 1].astype(F32)
        before, after = half_pads(last, head)
        pp_ref[k, 0, 1 : nz + 1] = before.astype(BF16)
        pp_ref[k, ny + 1, 1 : nz + 1] = after.astype(BF16)

        def zero_ends(y, carry, k=k):
            pp_ref[k, y, 0] = zero
            pp_ref[k, y, nz + 1] = zero
            return carry

        lax.fori_loop(0, ny + 2, zero_ends, 0)

    rows = 2 * nz * inner

    def conv(t, carry):
        xb = t // half
        y3 = t % half
        y = 2 * y3
        pieces = []
        for dy in range(3):
            for dz in range(3):
                for kk in range(2):
                    pieces.append(
                        pp_ref[xb + kk, pl.ds(y + dy, 2), dz : dz + nz].reshape(rows, LANES)
                    )
        out = dot(jnp.concatenate(pieces, axis=1), w_ref[...])
        sec_ref[xb, pl.ds(y, 2)] = out.reshape(2, nz, inner, 2 * LANES)
        act = leaky_relu(out)
        act = act[:, :LANES] + act[:, LANES:]
        act = act.reshape(2, nz // 2, 2, inner, LANES)
        act = (act[0, :, 0] + act[0, :, 1]) + (act[1, :, 0] + act[1, :, 1])
        act = (act * 0.125).astype(BF16).astype(F32)
        count = nz // 2 * inner
        start = pl.multiple_of((xb * half + y3) * count, count)
        ft[pl.ds(start, count), :] = act.reshape(count, LANES)
        return carry

    nxb = planes // 2
    lax.fori_loop(0, nxb * half, conv, 0)

    per_half = half * (nz // 2)

    def turn(s, carry):
        parts = []
        for xb in range(nxb):
            for h in range(HALVES):
                start = xb * per_half * inner + h * samples + s
                parts.append(ft[pl.ds(start, per_half, stride=inner), :])
        turned = jnp.concatenate(parts, axis=0).T
        fcs[pl.ds(s, channels, stride=samples), 0:cells] = turned
        return carry

    lax.fori_loop(0, samples, turn, 0)
    fc_ref[...] = fcs[:, 0:cells].reshape(channels, samples, cells).astype(BF16)

    def dense(t, acc):
        for u in range(8):
            ch = t * 8 + u
            acc[u % 4] = acc[u % 4] + dot(fc_ref[ch], d_ref[ch, 0])
        return acc

    zeros = [jnp.zeros((samples, LANES), F32) for _ in range(4)]
    acc = lax.fori_loop(0, channels // 8, dense, zeros)
    hid_ref[...] = (acc[0] + acc[1]) + (acc[2] + acc[3])


def second_conv(j, pd, lo, hi, w2, dense4, samples):
    planes, ny, nz, inner, _ = pd.shape
    channels, spaces, cells, units = dense4.shape
    pairs = planes // 2 + 1
    nxb = planes // 2
    pp_shape = (pairs, ny + 2, nz + 2, inner, LANES)
    sec_shape = (nxb, ny, nz, inner, 2 * LANES)
    fc_shape = (channels, samples, cells)

    def const(shape):
        return pl.BlockSpec(shape, lambda i, j_ref: (0,) * len(shape), pipeline_mode=pl.Buffered(1))

    return call(
        lambda *refs: second_kernel(samples, *refs),
        (
            jax.ShapeDtypeStruct(pp_shape, BF16),
            jax.ShapeDtypeStruct(sec_shape, F32),
            jax.ShapeDtypeStruct(fc_shape, BF16),
            jax.ShapeDtypeStruct((samples, units), F32),
        ),
        grid_spec=pltpu.PrefetchScalarGridSpec(
            num_scalar_prefetch=1,
            grid=(1,),
            in_specs=[const(pd.shape), const(lo.shape), const(hi.shape), const(w2.shape),
                      pl.BlockSpec((channels, 1, cells, units), lambda i, j_ref: (0, j_ref[0], 0, 0), pipeline_mode=pl.Buffered(1))],
            out_specs=(const(pp_shape), const(sec_shape), const(fc_shape), const((samples, units))),
            scratch_shapes=[
                pltpu.VMEM((nxb * (ny // 2) * (nz // 2) * inner, LANES), F32),
                pltpu.VMEM((channels * samples, LANES), F32),
            ],
        ),
        name="second_conv",
    )(j, pd, lo, hi, w2, dense4)


def dense_kernel(samples, own, targets_n, j_ref, hp_ref, tg_ref, do_ref, d_ref, sec_ref,
                 pred_ref, bh_ref, gdo_ref, bs_ref, bfc, bf):
    nxb, ny, nz, inner, _ = sec_ref.shape
    channels = d_ref.shape[0]
    cells = d_ref.shape[2]
    hp = hp_ref[...]
    hidden = leaky_relu(hp).astype(BF16).astype(F32)
    row = lax.broadcasted_iota(jnp.int32, (samples, 1), 0)
    mine = (row // own) == j_ref[0]
    lane = lax.broadcasted_iota(jnp.int32, (samples, LANES), 1)
    preds = jnp.zeros((samples, LANES), F32)
    back = jnp.zeros_like(hp)
    for t in range(targets_n):
        weight = do_ref[t : t + 1, :]
        pred = jnp.sum(hidden * weight, axis=1, keepdims=True)
        misfit = pred - tg_ref[:, t : t + 1]
        preds = jnp.where(lane == t, pred, preds)
        gdo_ref[t : t + 1, :] = jnp.sum(jnp.where(mine, hidden * misfit, 0.0), axis=0, keepdims=True)
        back = back + misfit * weight
    pred_ref[...] = preds
    bh = (back * slope_of(hp)).astype(BF16)
    bh_ref[...] = bh

    def features(t, carry):
        for u in range(8):
            ch = t * 8 + u
            out = dot_lanes(bh, d_ref[ch, 0])
            bfc[pl.ds(pl.multiple_of(ch * samples, samples), samples), 0:cells] = out
        return carry

    lax.fori_loop(0, channels // 8, features, 0)
    half = ny // 2
    per_half = half * (nz // 2)

    def turn(s, carry):
        turned = bfc[pl.ds(s, channels, stride=samples), 0:cells].T
        for xb in range(nxb):
            for h in range(HALVES):
                start = xb * per_half * inner + h * samples + s
                at = (xb * HALVES + h) * per_half
                bf[pl.ds(start, per_half, stride=inner), :] = turned[at : at + per_half]
        return carry

    lax.fori_loop(0, samples, turn, 0)
    count = nz // 2 * inner

    def spread(t, carry):
        xb = t // half
        y3 = t % half
        start = pl.multiple_of(t * count, count)
        g = bf[pl.ds(start, count), :].reshape(nz // 2, 1, inner, LANES) * 0.125
        g = jnp.broadcast_to(g, (nz // 2, 2, inner, LANES)).reshape(nz, inner, LANES)
        for dy in range(2):
            y = 2 * y3 + dy
            slope = slope_of(sec_ref[xb, y])
            for px in range(2):
                bs_ref[2 * xb + px, y] = (g * slope[:, :, px * LANES : (px + 1) * LANES]).astype(BF16)
        return carry

    lax.fori_loop(0, nxb * half, spread, 0)


def dense_layers(j, hp, targets, dense_out_t, dense4, sec, own):
    nxb, ny, nz, inner, _ = sec.shape
    channels, spaces, cells, units = dense4.shape
    samples, targets_n = targets.shape
    bs_shape = (2 * nxb, ny, nz, inner, LANES)

    def const(shape):
        return pl.BlockSpec(shape, lambda i, j_ref: (0,) * len(shape), pipeline_mode=pl.Buffered(1))

    return call(
        lambda *refs: dense_kernel(samples, own, targets_n, *refs),
        (
            jax.ShapeDtypeStruct((samples, LANES), F32),
            jax.ShapeDtypeStruct((samples, units), BF16),
            jax.ShapeDtypeStruct((targets_n, units), F32),
            jax.ShapeDtypeStruct(bs_shape, BF16),
        ),
        grid_spec=pltpu.PrefetchScalarGridSpec(
            num_scalar_prefetch=1,
            grid=(1,),
            in_specs=[const(hp.shape), const(targets.shape), const(dense_out_t.shape),
                      pl.BlockSpec((channels, 1, cells, units), lambda i, j_ref: (0, j_ref[0], 0, 0), pipeline_mode=pl.Buffered(1)),
                      const(sec.shape)],
            out_specs=(const((samples, LANES)), const((samples, units)), const((targets_n, units)), const(bs_shape)),
            scratch_shapes=[
                pltpu.VMEM((channels * samples, LANES), F32),
                pltpu.VMEM((nxb * (ny // 2) * (nz // 2) * inner, LANES), F32),
            ],
        ),
        name="dense_layers",
    )(j, hp, targets, dense_out_t, dense4, sec)


def dense_grad_kernel(f_ref, b_ref, o_ref):
    groups, spaces, chans, samples, cells = f_ref.shape
    b = b_ref[...].astype(F32).reshape(groups * samples, b_ref.shape[2]).astype(BF16)
    for ch in range(chans):
        for j in range(spaces):
            f = f_ref[:, j, ch].astype(F32).reshape(groups * samples, cells).astype(BF16)
            o_ref[ch, j] = dot_rows(f, b)


def dense_grad(feats, bh):
    groups, spaces, chans, samples, cells = feats.shape
    shape = (chans, spaces, cells, bh.shape[2])
    return call(dense_grad_kernel, jax.ShapeDtypeStruct(shape, F32), name="dense_grad")(feats, bh)


def second_grad_kernel(bs_ref, pp_ref, g_ref, acc):
    planes, ny, nz, inner, _ = bs_ref.shape
    nxb = planes // 2
    half = ny // 2
    rows = 2 * nz * inner
    acc[...] = jnp.zeros_like(acc)

    def step(t, carry):
        xb = t // half
        y = 2 * (t % half)
        left = jnp.concatenate(
            [bs_ref[2 * xb + px, pl.ds(y, 2)].reshape(rows, LANES) for px in range(2)], axis=1
        ).T
        for dy in range(3):
            for dz in range(3):
                right = jnp.concatenate(
                    [
                        pp_ref[xb + kk, pl.ds(y + dy, 2), dz : dz + nz].reshape(rows, LANES)
                        for kk in range(2)
                    ],
                    axis=1,
                )
                acc[dy * 3 + dz] = acc[dy * 3 + dz] + dot(left, right)
        return carry

    lax.fori_loop(0, nxb * half, step, 0)
    mid = LANES // 2
    for o in range(9):
        both = acc[o, :LANES, 0 : 3 * mid] + acc[o, LANES:, mid : 4 * mid]
        for a in range(3):
            at = (a * 9 + o) * mid
            g_ref[:, at : at + mid] = both[:, a * mid : (a + 1) * mid]


def second_grad(bs, pp):
    return call(
        second_grad_kernel,
        jax.ShapeDtypeStruct((LANES, 27 * LANES // 2), F32),
        scratch_shapes=[pltpu.VMEM((9, 2 * LANES, 2 * LANES), F32)],
        name="second_grad",
    )(bs, pp)


def second_back_kernel(bs_ref, lo_ref, hi_ref, w_ref, bp_ref, pad):
    planes, ny, nz, inner, _ = bs_ref.shape
    nxb = planes // 2
    zero = jnp.zeros((inner, LANES), BF16)
    for p in range(planes + 2):

        def fill(y, carry, p=p):
            if p == 0:
                v = lo_ref[y]
            elif p == planes + 1:
                v = hi_ref[y]
            else:
                v = bs_ref[p - 1, y]
            pad[p, y + 1, 1 : nz + 1] = v
            return carry

        lax.fori_loop(0, ny, fill, 0)
        before, after = half_pads(
            pad[p, ny, 1 : nz + 1].astype(F32), pad[p, 1, 1 : nz + 1].astype(F32)
        )
        pad[p, 0, 1 : nz + 1] = before.astype(BF16)
        pad[p, ny + 1, 1 : nz + 1] = after.astype(BF16)

        def zero_ends(y, carry, p=p):
            pad[p, y, 0] = zero
            pad[p, y, nz + 1] = zero
            return carry

        lax.fori_loop(0, ny + 2, zero_ends, 0)

    quarter = ny // 4
    rows = nz * inner
    depth = 16 * LANES

    def step(t, carry):
        xb = t // quarter
        y = 4 * (t % quarter)
        out = jnp.zeros((2 * rows, 2 * LANES), F32)
        for dz in range(3):
            pieces = []
            for jx in range(4):
                for jy in range(4):
                    pieces.append(
                        jnp.concatenate(
                            [
                                pad[2 * xb + jx, y + 2 * u + jy, dz : dz + nz].reshape(rows, LANES)
                                for u in range(2)
                            ],
                            axis=0,
                        )
                    )
            out = out + dot(
                jnp.concatenate(pieces, axis=1), w_ref[dz * depth : (dz + 1) * depth, :]
            )
        out = out.astype(BF16).astype(F32)
        mask = low_half((2 * rows, LANES))
        for px in range(2):
            v = out[:, px * LANES : (px + 1) * LANES]
            r = roll_half(v)
            for py in range(2):
                d = jnp.where(mask, v, r) if py == 0 else jnp.where(mask, r, v)
                d = d.astype(BF16).reshape(2, nz, inner, LANES)
                for u in range(2):
                    bp_ref[2 * xb + px, y + 2 * u + py] = d[u]
        return carry

    lax.fori_loop(0, nxb * quarter, step, 0)


def second_back(bs, lo, hi, w3):
    planes, ny, nz, inner, _ = bs.shape
    return call(
        second_back_kernel,
        jax.ShapeDtypeStruct(bs.shape, BF16),
        scratch_shapes=[pltpu.VMEM((planes + 2, ny + 2, nz + 2, inner, LANES), BF16)],
        name="second_back",
    )(bs, lo, hi, w3)


def active_of(f, bp, mean, inverse, gain, shift):
    nz, inner, _ = f.shape
    w = (f.reshape(nz * inner, 2 * LANES) - mean) * inverse
    slope = slope_of(gain * w + shift)
    g = bp.astype(F32).reshape(nz // 2, 1, inner, LANES) * 0.125
    g = jnp.broadcast_to(g, (nz // 2, 2, inner, LANES)).reshape(nz * inner, LANES)
    return w, slope * jnp.concatenate([g, g], axis=1)


def sums_kernel(local_count, total_count, f_ref, bp_ref, st_ref, gs_ref, o_ref, acc):
    i = pl.program_id(0)
    mean, inverse = group_stats(st_ref[...], local_count, total_count)
    mean, inverse = wide(mean), wide(inverse)
    gain, shift = wide(gs_ref[0:1]), wide(gs_ref[1:2])

    @pl.when(i == 0)
    def _():
        acc[...] = jnp.zeros_like(acc)

    def step(yb, carry):
        w, active = active_of(f_ref[0, yb], bp_ref[0, yb], mean, inverse, gain, shift)
        acc[0] = acc[0] + jnp.sum((active * w).reshape(-1, 8, 2 * LANES), axis=0)
        acc[1] = acc[1] + jnp.sum(active.reshape(-1, 8, 2 * LANES), axis=0)
        return carry

    lax.fori_loop(0, f_ref.shape[1], step, 0)

    @pl.when(i == pl.num_programs(0) - 1)
    def _():
        rows = [jnp.sum(acc[k], axis=0, keepdims=True) for k in range(2)]
        rows = [both_halves(r[:, :LANES] + r[:, LANES:]) for r in rows]
        o_ref[...] = jnp.concatenate(rows, axis=0)


def norm_sums(f, bp, st, gs, local_count, total_count):
    return call(
        lambda *refs: sums_kernel(local_count, total_count, *refs),
        jax.ShapeDtypeStruct((2, LANES), F32),
        grid=(f.shape[0],),
        in_specs=[
            pl.BlockSpec((1,) + f.shape[1:], lambda i: (i, 0, 0, 0, 0)),
            pl.BlockSpec((1,) + bp.shape[1:], lambda i: (i, 0, 0, 0, 0)),
            whole_spec(st.shape),
            whole_spec(gs.shape),
        ],
        out_specs=whole_spec((2, LANES)),
        scratch_shapes=[pltpu.VMEM((2, 8, 2 * LANES), F32)],
        name="norm_sums",
    )(f, bp, st, gs)


def first_grad_kernel(local_count, total_count, c, f_ref, bp_ref, st_ref, gs_ref, sum_ref, xa_ref, xc_ref, g_ref, acc):
    i = pl.program_id(0)
    mean, inverse = group_stats(st_ref[...], local_count, total_count)
    mean, inverse = wide(mean), wide(inverse)
    gain, shift = wide(gs_ref[0:1]), wide(gs_ref[1:2])
    cross = wide(sum_ref[0:1]) * (1.0 / total_count)
    plain = wide(sum_ref[1:2]) * (1.0 / total_count)
    scale = gain * inverse
    nz = f_ref.shape[2]
    inner = f_ref.shape[3]
    rows = nz * inner

    @pl.when(i == 0)
    def _():
        acc[...] = jnp.zeros_like(acc)

    def step(yb, carry):
        w, active = active_of(f_ref[0, yb], bp_ref[0, yb], mean, inverse, gain, shift)
        left = (scale * (active - plain - w * cross)).astype(BF16).T
        for dz in range(3):
            for kk, x_ref in enumerate((xa_ref, xc_ref)):
                right = jnp.concatenate(
                    [x_ref[0, yb + mm, dz : dz + nz].reshape(rows, LANES) for mm in range(2)],
                    axis=1,
                )
                acc[dz * 2 + kk] = acc[dz * 2 + kk] + dot(left, right)
        return carry

    lax.fori_loop(0, f_ref.shape[1], step, 0)

    @pl.when(i == pl.num_programs(0) - 1)
    def _():
        co = LANES // 2
        for a in range(3):
            for b in range(3):
                for d in range(3):
                    total = None
                    for px in range(2):
                        for py in range(2):
                            xw, yw = a + px, b + py
                            at = (yw // 2) * LANES + (yw % 2) * 2 * c + (xw % 2) * c
                            top = (px * 2 + py) * co
                            part = acc[d * 2 + xw // 2, top : top + co, at : at + c]
                            total = part if total is None else total + part
                    at = ((a * 3 + b) * 3 + d) * c
                    g_ref[:, at : at + c] = total


def first_grad(f, bp, st, gs, sums, xb, c, local_count, total_count):
    x_block = (1,) + xb.shape[1:]
    out = (LANES // 2, 27 * c)
    return call(
        lambda *refs: first_grad_kernel(local_count, total_count, c, *refs),
        jax.ShapeDtypeStruct(out, F32),
        grid=(f.shape[0],),
        in_specs=[
            pl.BlockSpec((1,) + f.shape[1:], lambda i: (i, 0, 0, 0, 0)),
            pl.BlockSpec((1,) + bp.shape[1:], lambda i: (i, 0, 0, 0, 0)),
            whole_spec(st.shape),
            whole_spec(gs.shape),
            whole_spec(sums.shape),
            pl.BlockSpec(x_block, lambda i: (i, 0, 0, 0, 0)),
            pl.BlockSpec(x_block, lambda i: (i + 1, 0, 0, 0, 0)),
        ],
        out_specs=whole_spec(out),
        scratch_shapes=[pltpu.VMEM((6, 2 * LANES, 2 * LANES), F32)],
        name="first_grad",
    )(f, bp, st, gs, sums, xb, xb)


def swap_edges(first, last, axis):
    count = lax.axis_size(axis)
    before = lax.ppermute(last, axis, [(i, i + 1) for i in range(count - 1)])
    after = lax.ppermute(first, axis, [(i + 1, i) for i in range(count - 1)])
    return before, after


def shards(inputs, conv_in, norm_gain, norm_shift, conv_out, dense_in, dense_out, targets):
    samples, c, planes, cells = inputs.shape
    spaces = lax.axis_size("space")
    groups = lax.axis_size("dp")
    units = dense_in.shape[1]
    channels = conv_out.shape[0]
    own = targets.shape[0]
    local_count = float(samples * planes * cells)
    total_count = local_count * spaces

    before, after = swap_edges(inputs[:, :, :1], inputs[:, :, planes - 1 :], "space")
    halo = jnp.concatenate([before, after], axis=1).reshape(samples, 2 * c, cells)
    w1 = first_weights(conv_in)
    w2 = second_weights(conv_out)
    w3 = adjoint_weights(conv_out)
    gs = jnp.stack([norm_gain, norm_shift])
    gs = jnp.concatenate([gs, gs], axis=1)
    j = lax.axis_index("space").astype(jnp.int32).reshape(1)
    dense4 = dense_in.reshape(channels, spaces, dense_in.shape[0] // (channels * spaces), units)
    group_targets = lax.all_gather(targets, "space", axis=0, tiled=True)

    f, xb, st = first_conv(inputs.reshape(samples, c * planes, cells), halo, w1, planes)
    stats = lax.all_gather(st, "space")
    pd, edge_lo, edge_hi = normalise_pool(f, stats, gs, local_count, total_count)
    lo, hi = swap_edges(edge_lo, edge_hi, "space")
    pp, sec, fc, partial = second_conv(j, pd, lo, hi, w2, dense4, samples)
    hp = lax.psum(partial, "space")
    preds, bh, gdo, bs = dense_layers(
        j, hp, group_targets, dense_out.astype(F32).T, dense4, sec, own
    )
    everyone = groups * spaces
    sent = fc.reshape((everyone, channels // everyone) + fc.shape[1:])
    feats = lax.all_to_all(sent, ("dp", "space"), split_axis=0, concat_axis=0, tiled=True)
    feats = feats.reshape((groups, spaces) + sent.shape[1:])
    all_bh = lax.all_gather(bh, "dp")
    bs_lo, bs_hi = swap_edges(bs[0], bs[-1], "space")
    grad_conv_out = lax.psum(second_grad(bs, pp), ("dp", "space"))
    bp = second_back(bs, bs_lo, bs_hi, w3)
    sums = norm_sums(f, bp, stats, gs, local_count, total_count)
    group_sums = lax.psum(sums, "space")
    grad_dense_in = dense_grad(feats, all_bh).reshape(-1, units)
    grad_conv_in = first_grad(f, bp, stats, gs, group_sums, xb, c, local_count, total_count)
    grad_conv_in, sums, gdo = lax.psum((grad_conv_in, sums, gdo), ("dp", "space"))
    first_row = lax.axis_index("space") * own
    predictions = lax.dynamic_slice_in_dim(preds, first_row, own, axis=0)[:, : targets.shape[1]]
    return (
        grad_conv_in,
        sums[:, : norm_gain.shape[0]],
        grad_conv_out,
        grad_dense_in,
        gdo.T,
        predictions,
    )


def solution(mesh):
    placed = (P("dp", None, "space", None), P(), P(), P(), P(), P(), P(), P(("dp", "space"), None))
    return jax.shard_map(
        shards,
        mesh=mesh,
        in_specs=placed,
        out_specs=(P(), P(), P(), P(("dp", "space"), None), P(), P(("dp", "space"), None)),
        check_vma=False,
    )
```

```python
import jax
import jax.numpy as jnp
import numpy as np
from jax import lax
from jax.experimental import pallas as pl
from jax.experimental.pallas import tpu as pltpu
from jax.sharding import PartitionSpec as P


GRID = 32
HALVES = 2
LANES = 128
norm_epsilon = 1e-05
INTERPRET = False

F32 = jnp.float32
BF16 = jnp.bfloat16


def leaky_relu(values):
    return values * (0.65 + 0.35 * jnp.tanh(values))


def slope_of(values):
    bent = jnp.tanh(values)
    return 0.65 + 0.35 * (bent + values * (1.0 - bent * bent))


def dot(a, b):
    return jnp.dot(a, b, preferred_element_type=F32)


def dot_rows(a, b):
    return lax.dot_general(a, b, (((0,), (0,)), ((), ())), preferred_element_type=F32)


def dot_lanes(a, b):
    return lax.dot_general(a, b, (((1,), (1,)), ((), ())), preferred_element_type=F32)


def low_half(shape):
    return lax.broadcasted_iota(jnp.int32, shape, len(shape) - 1) < LANES // 2


def roll_half(values):
    flat = values.reshape(-1, LANES)
    return pltpu.roll(flat, LANES // 2, 1).reshape(values.shape)


def both_halves(values):
    return values + roll_half(values)


def call(kernel, out_shape, cost_us=1.0, **kwargs):
    cost = pl.CostEstimate(
        flops=int(cost_us * 1e9), bytes_accessed=int(cost_us * 3e6), transcendentals=0
    )
    return pl.pallas_call(
        kernel, out_shape=out_shape, interpret=INTERPRET, cost_estimate=cost, **kwargs
    )


def whole_spec(shape):
    return pl.BlockSpec(shape, lambda *_: (0,) * len(shape), pipeline_mode=pl.Buffered(1))


def weights_kernel(c_in, c_mid, ci_ref, co_ref, w1_ref, w2_ref, v3_ref, t1, t2):
    def offset(a, b, d):
        return (a * 3 + b) * 3 + d

    for k in range(ci_ref.shape[1] // LANES):
        lanes = slice(k * LANES, (k + 1) * LANES)
        t1[lanes, :] = both_halves(ci_ref[:, lanes].astype(F32).T)
    for k in range(co_ref.shape[1] // LANES):
        lanes = slice(k * LANES, (k + 1) * LANES)
        t2[lanes, :] = co_ref[:, lanes].astype(F32).T
    mask = low_half((c_in, LANES))
    zero = jnp.zeros((c_in, LANES), F32)
    row = 0
    for d in range(3):
        for kk in range(2):
            for mm in range(2):
                for yo in range(2):
                    for xo in range(2):
                        for px in range(2):
                            a = 2 * kk + xo - px
                            parts = []
                            for py in range(2):
                                b = 2 * mm + yo - py
                                if 0 <= a <= 2 and 0 <= b <= 2:
                                    at = offset(a, b, d) * c_in
                                    parts.append(t1[at : at + c_in, :])
                                else:
                                    parts.append(zero)
                            w1_ref[row : row + c_in, px * LANES : (px + 1) * LANES] = jnp.where(
                                mask, parts[0], parts[1]
                            ).astype(BF16)
                        row += c_in
    row = 0
    for b in range(3):
        for d in range(3):
            for xw in range(4):
                for px in range(2):
                    a = xw - px
                    if 0 <= a <= 2:
                        at = offset(a, b, d) * c_mid
                        part = t2[at : at + c_mid, :].astype(BF16)
                    else:
                        part = jnp.zeros((c_mid, LANES), BF16)
                    w2_ref[row : row + c_mid, px * LANES : (px + 1) * LANES] = part
                row += c_mid
    mask = low_half((LANES, LANES))
    zero = jnp.zeros((LANES, LANES), F32)
    for d in range(3):
        for a in range(3):
            for yw in range(4):
                parts = []
                for py in range(2):
                    b = yw - py
                    if 0 <= b <= 2:
                        o = offset(2 - a, 2 - b, 2 - d)
                        v = co_ref[:, o // 2 * LANES : (o // 2 + 1) * LANES].astype(F32)
                        parts.append(v if o % 2 == py else roll_half(v))
                    else:
                        parts.append(zero)
                v3_ref[d, a, yw] = jnp.where(mask, parts[0], parts[1]).astype(BF16)


def make_weights(conv_in, conv_out):
    c_in = conv_in.shape[1] // 27
    c_mid = conv_out.shape[1] // 27
    wide_in = -(-conv_in.shape[1] // LANES) * LANES
    wide_out = -(-conv_out.shape[1] // LANES) * LANES
    ci = jnp.pad(conv_in, ((0, LANES - conv_in.shape[0]), (0, wide_in - conv_in.shape[1])))
    co = jnp.pad(conv_out, ((0, 0), (0, wide_out - conv_out.shape[1])))
    return call(
        lambda *refs: weights_kernel(c_in, c_mid, *refs),
        (
            jax.ShapeDtypeStruct((48 * c_in, 2 * LANES), BF16),
            jax.ShapeDtypeStruct((36 * c_mid, 2 * LANES), BF16),
            jax.ShapeDtypeStruct((3, 3, 4, LANES, LANES), BF16),
        ),
        5.0,
        scratch_shapes=[pltpu.VMEM((wide_in, LANES), F32), pltpu.VMEM((wide_out, LANES), F32)],
        name="weights",
    )(ci, co)


def half_pads(before, after):
    zero = jnp.zeros_like(before[:, 0:8])
    return (
        jnp.concatenate([zero, before[:, 0:8]], axis=1),
        jnp.concatenate([after[:, 8:16], zero], axis=1),
    )


def gather_rows(src_ref, sel_ref, z_ref, samples):
    half_y = GRID // HALVES
    chunks = z_ref.shape[0]
    inner = HALVES * samples
    groups = GRID * GRID // LANES
    per_group = LANES // GRID

    def gather(t, carry):
        s = t % samples
        q = t // samples
        for h in range(HALVES):
            g = q + h * (groups // HALVES)
            lanes = pl.ds(pl.multiple_of(g * LANES, LANES), LANES)
            val = dot_rows(src_ref[s, :, lanes], sel_ref[...])
            start = (per_group * q + 1) * GRID * inner + h * samples + s
            for k in range(chunks):
                z_ref[k, pl.ds(start, LANES, stride=inner), :] = val[:, k * LANES : (k + 1) * LANES]
        return carry

    lax.fori_loop(0, samples * groups // HALVES, gather, 0)
    row = GRID * inner
    for k in range(chunks):
        last = plane_of(z_ref, k, half_y, row).reshape(GRID, inner, LANES)
        head = plane_of(z_ref, k, 1, row).reshape(GRID, inner, LANES)
        lo, hi = half_pads(last, head)
        z_ref[k, 0:row, :] = lo.reshape(row, LANES)
        z_ref[k, (half_y + 1) * row : (half_y + 2) * row, :] = hi.reshape(row, LANES)


def plane_of(z_ref, k, y, row):
    return z_ref[k, pl.ds(pl.multiple_of(y * row, row), row), :]


def prepare_kernel(planes, samples, x_ref, pa_ref, xb_ref, z_ref):
    pairs = planes // 2 + 1
    half_y = GRID // HALVES
    inner = HALVES * samples
    row = GRID * inner
    gather_rows(x_ref, pa_ref, z_ref, samples)

    def assemble(m, carry):
        mask = low_half((row, LANES))
        for k in range(pairs):
            a = plane_of(z_ref, k // 2, 2 * m, row)
            b = plane_of(z_ref, k // 2, 2 * m + 1, row)
            if k % 2 == 0:
                b = roll_half(b)
            else:
                a = roll_half(a)
            both = jnp.where(mask, a, b).astype(BF16)
            xb_ref[k, m, 1 : GRID + 1] = both.reshape(GRID, inner, LANES)
            zero = jnp.zeros((inner, LANES), BF16)
            xb_ref[k, m, 0] = zero
            xb_ref[k, m, GRID + 1] = zero
        return carry

    lax.fori_loop(0, half_y // 2 + 1, assemble, 0)


def prepare(x, planes, c):
    samples = x.shape[0]
    pairs = planes // 2 + 1
    chunks = -(-pairs * 2 * c // LANES)
    inner = HALVES * samples
    half_y = GRID // HALVES
    pa = np.zeros((c * planes, chunks * LANES), np.float32)
    for ch in range(c):
        for p in range(planes):
            pa[ch * planes + p, (p + 1) * c + ch] = 1.0
    return call(
        lambda *refs: prepare_kernel(planes, samples, *refs),
        jax.ShapeDtypeStruct((pairs, half_y // 2 + 1, GRID + 2, inner, LANES), BF16),
        20.0,
        scratch_shapes=[pltpu.VMEM((chunks, (half_y + 2) * GRID * inner, LANES), F32)],
        name="prepare",
    )(x, jnp.asarray(pa, BF16))


def first_kernel(planes, samples, refs):
    (xi_ref, halo_ref, pb_ref, w_ref, f_ref, xb_ref, st_ref, z_ref, w_acc) = refs
    i = pl.program_id(0)
    pairs = planes // 2 + 1
    half_y = GRID // HALVES
    inner = HALVES * samples
    rows = GRID * inner
    blocks = half_y // 2
    per_block = rows // 8

    @pl.when(i == 0)
    def _():
        gather_rows(halo_ref, pb_ref, z_ref, samples)

        def patch(m, carry):
            lane = lax.broadcasted_iota(jnp.int32, (rows, LANES), 1)
            a = plane_of(z_ref, 0, 2 * m, rows)
            b = plane_of(z_ref, 0, 2 * m + 1, rows)
            edge = jnp.where(lane < LANES // 2, a, b)
            first = lane % (LANES // 2) < LANES // 4
            for k in range(pairs):
                xb_ref[k, m] = xi_ref[k, m]
            for k in (0, pairs - 1):
                own = xi_ref[k, m, 1 : GRID + 1].astype(F32).reshape(rows, LANES)
                both = jnp.where(first, edge, own) if k == 0 else jnp.where(first, own, edge)
                xb_ref[k, m, 1 : GRID + 1] = both.astype(BF16).reshape(GRID, inner, LANES)
            return carry

        lax.fori_loop(0, blocks + 1, patch, 0)
        w_acc[...] = jnp.zeros_like(w_acc)

    def conv(yb, carry):
        pieces = []
        for dz in range(3):
            for kk in range(2):
                for mm in range(2):
                    pieces.append(
                        xb_ref[i + kk, yb + mm, dz : dz + GRID].reshape(rows, LANES)
                    )
        out = dot(jnp.concatenate(pieces, axis=1), w_ref[...])
        f_ref[0, yb] = out.reshape(GRID, inner, 2 * LANES)
        stacked = out.reshape(per_block, 8, 2 * LANES)
        mean = jnp.sum(stacked, axis=0) * (1.0 / per_block)
        dev = stacked - mean[None]
        square = jnp.sum(dev * dev, axis=0)
        done = (i * blocks + yb).astype(F32)
        delta = mean - w_acc[0]
        w_acc[0] = w_acc[0] + delta / (done + 1.0)
        w_acc[1] = w_acc[1] + square + delta * delta * (per_block * done / (done + 1.0))
        return carry

    lax.fori_loop(0, blocks, conv, 0)

    @pl.when(i == pl.num_programs(0) - 1)
    def _():
        count = float(per_block * blocks * (planes // 2))
        mean = w_acc[0]
        m = jnp.mean(mean, axis=0, keepdims=True)
        m = both_halves((m[:, :LANES] + m[:, LANES:]) * 0.5) * 0.5
        dev = mean - wide(m)
        q = jnp.sum(w_acc[1] + count * dev * dev, axis=0, keepdims=True)
        q = both_halves(q[:, :LANES] + q[:, LANES:])
        st = jnp.concatenate([m, q], axis=0)
        st_ref[...] = st


def first_conv(xi, halo, w1, planes):
    samples = halo.shape[0]
    c = halo.shape[1] // 2
    inner = HALVES * samples
    half_y = GRID // HALVES
    pb = np.zeros((2 * c, LANES), np.float32)
    for ch in range(2 * c):
        pb[ch, ch] = 1.0
        pb[ch, LANES // 2 + ch] = 1.0
    pb = jnp.asarray(pb, BF16)
    nxb = planes // 2
    f_shape = (nxb, half_y // 2, GRID, inner, 2 * LANES)
    return call(
        lambda *refs: first_kernel(planes, samples, refs),
        (
            jax.ShapeDtypeStruct(f_shape, F32),
            jax.ShapeDtypeStruct(xi.shape, BF16),
            jax.ShapeDtypeStruct((2, LANES), F32),
        ),
        25.0,
        grid=(nxb,),
        in_specs=[whole_spec(a.shape) for a in (xi, halo, pb, w1)],
        out_specs=(
            pl.BlockSpec((1,) + f_shape[1:], lambda i: (i, 0, 0, 0, 0)),
            whole_spec(xi.shape),
            whole_spec((2, LANES)),
        ),
        scratch_shapes=[
            pltpu.VMEM((1, (half_y + 2) * GRID * inner, LANES), F32),
            pltpu.VMEM((2, 8, 2 * LANES), F32),
        ],
        name="first_conv",
    )(xi, halo, pb, w1)


def group_stats(st, local_count, total_count):
    means = st[:, 0]
    mean = jnp.mean(means, axis=0, keepdims=True)
    dev = means - mean
    square = jnp.sum(st[:, 1] + local_count * dev * dev, axis=0, keepdims=True)
    inverse = lax.rsqrt(square / total_count + norm_epsilon)
    return mean, inverse


def wide(row):
    return jnp.concatenate([row, row], axis=1)


def pool_kernel(local_count, total_count, f_ref, st_ref, gs_ref, pd_ref, edge_ref=None):
    mean, inverse = group_stats(st_ref[...], local_count, total_count)
    mean = wide(mean)
    inverse = wide(inverse)
    gain = wide(gs_ref[0:1])
    shift = wide(gs_ref[1:2])
    nyb = f_ref.shape[1]
    nz = f_ref.shape[2]
    inner = f_ref.shape[3]

    def step(yb, carry):
        f = f_ref[0, yb].reshape(nz * inner, 2 * LANES)
        act = leaky_relu(gain * ((f - mean) * inverse) + shift)
        act = act[:, :LANES] + act[:, LANES:]
        act = act.reshape(nz // 2, 2, inner, LANES)
        act = act[:, 0] + act[:, 1]
        pooled = both_halves(act) * 0.125
        pd_ref[0, yb] = pooled.astype(BF16)
        return carry

    lax.fori_loop(0, nyb, step, 0)
    if edge_ref is not None:
        half = nyb // 2
        mask = low_half((nz // 2, inner, LANES))
        for y in range(half):
            edge_ref[0, y] = jnp.where(
                mask, pd_ref[0, y].astype(F32), pd_ref[0, y + half].astype(F32)
            ).astype(BF16)


def normalise_pool(f, st, gs, local_count, total_count, edges):
    nxb, nyb, nz, inner, _ = f.shape
    count = 2 if edges else nxb - 2
    stride, base = (nxb - 1, 0) if edges else (1, 1)
    pd_shape = (count, nyb, nz // 2, inner, LANES)
    edge = (2, nyb // 2, nz // 2, inner, LANES)
    shapes = [jax.ShapeDtypeStruct(pd_shape, BF16)]
    specs = [pl.BlockSpec((1,) + pd_shape[1:], lambda i: (i, 0, 0, 0, 0))]
    if edges:
        shapes.append(jax.ShapeDtypeStruct(edge, BF16))
        specs.append(pl.BlockSpec((1,) + edge[1:], lambda i: (i, 0, 0, 0, 0)))
    return call(
        lambda *refs: pool_kernel(local_count, total_count, *refs),
        shapes,
        3.0 * count,
        grid=(count,),
        in_specs=[
            pl.BlockSpec((1,) + f.shape[1:], lambda i: (i * stride + base, 0, 0, 0, 0)),
            whole_spec(st.shape),
            whole_spec(gs.shape),
        ],
        out_specs=specs,
        name="pool_edges" if edges else "pool_inside",
    )(f, st, gs)


def second_kernel(samples, refs):
    (j_ref, pe_ref, *mid, lo_ref, hi_ref, w_ref, d_ref, tg_ref,
     pp_ref, sec_ref, fc_ref, hid_ref, ft, fcs) = refs
    edges, ny, nz, inner, _ = pe_ref.shape
    planes = edges + (mid[0].shape[0] if mid else 0)

    def plane(p, y):
        if p == 0 or p == planes - 1:
            return pe_ref[min(p, 1), y].astype(F32)
        return mid[0][p - 1, y].astype(F32)

    pairs = planes // 2 + 1
    half = ny // 2
    cells = fc_ref.shape[2]
    channels = fc_ref.shape[0]

    def unpack(ref, y):
        v = ref[y % half].astype(F32)
        return jnp.where(low_half(v.shape) == (y < half), v, roll_half(v))

    def assemble(y, carry):
        mask = low_half((nz, inner, LANES))
        for k in range(pairs):
            a = unpack(lo_ref, y) if k == 0 else plane(2 * k - 1, y)
            b = unpack(hi_ref, y) if k == pairs - 1 else plane(2 * k, y)
            pp_ref[k, y + 1, 1 : nz + 1] = jnp.where(mask, a, b).astype(BF16)
        return carry

    lax.fori_loop(0, ny, assemble, 0)
    zero = jnp.zeros((inner, LANES), BF16)
    for k in range(pairs):
        last = pp_ref[k, ny, 1 : nz + 1].astype(F32)
        head = pp_ref[k, 1, 1 : nz + 1].astype(F32)
        before, after = half_pads(last, head)
        pp_ref[k, 0, 1 : nz + 1] = before.astype(BF16)
        pp_ref[k, ny + 1, 1 : nz + 1] = after.astype(BF16)

        def zero_ends(y, carry, k=k):
            pp_ref[k, y, 0] = zero
            pp_ref[k, y, nz + 1] = zero
            return carry

        lax.fori_loop(0, ny + 2, zero_ends, 0)

    rows = 2 * nz * inner

    def conv(t, carry):
        xb = t // half
        y3 = t % half
        y = 2 * y3
        pieces = []
        for dy in range(3):
            for dz in range(3):
                for kk in range(2):
                    pieces.append(
                        pp_ref[xb + kk, pl.ds(y + dy, 2), dz : dz + nz].reshape(rows, LANES)
                    )
        out = dot(jnp.concatenate(pieces, axis=1), w_ref[...])
        sec_ref[xb, pl.ds(y, 2)] = out.reshape(2, nz, inner, 2 * LANES)
        act = leaky_relu(out)
        act = act[:, :LANES] + act[:, LANES:]
        act = act.reshape(2, nz // 2, 2, inner, LANES)
        act = (act[0, :, 0] + act[0, :, 1]) + (act[1, :, 0] + act[1, :, 1])
        act = (act * 0.125).astype(BF16).astype(F32)
        count = nz // 2 * inner
        start = pl.multiple_of((xb * half + y3) * count, count)
        ft[pl.ds(start, count), :] = act.reshape(count, LANES)
        return carry

    nxb = planes // 2
    lax.fori_loop(0, nxb * half, conv, 0)

    per_half = half * (nz // 2)

    def turn(s, carry):
        parts = []
        for xb in range(nxb):
            for h in range(HALVES):
                start = xb * per_half * inner + h * samples + s
                parts.append(ft[pl.ds(start, per_half, stride=inner), :])
        turned = jnp.concatenate(parts, axis=0).T
        fcs[pl.ds(s, channels, stride=samples), 0:cells] = turned
        return carry

    lax.fori_loop(0, samples, turn, 0)
    fc_ref[...] = fcs[:, 0:cells].reshape(channels, samples, cells).astype(BF16)

    def dense(t, acc):
        for u in range(8):
            ch = t * 8 + u
            acc[u % 4] = acc[u % 4] + dot(fc_ref[ch], d_ref[ch, 0])
        return acc

    zeros = [jnp.zeros((samples, LANES), F32) for _ in range(4)]
    acc = lax.fori_loop(0, channels // 8, dense, zeros)
    total = (acc[0] + acc[1]) + (acc[2] + acc[3])
    own, targets_n = tg_ref.shape
    hid_ref[0:samples] = total
    hid_ref[samples : 2 * samples] = jnp.zeros_like(total)
    for q in range(own):
        at = samples + j_ref[0] * own + q
        hid_ref[pl.ds(at, 1), 0:targets_n] = tg_ref[q : q + 1, :]


def second_conv(j, pds, lo, hi, w2, dense4, targets, samples):
    _, ny, nz, inner, _ = pds[0].shape
    planes = sum(p.shape[0] for p in pds)
    channels, _, cells, units = dense4.shape
    pairs = planes // 2 + 1
    nxb = planes // 2
    pp_shape = (pairs, ny + 2, nz + 2, inner, LANES)
    sec_shape = (nxb, ny, nz, inner, 2 * LANES)
    fc_shape = (channels, samples, cells)

    def const(shape):
        return pl.BlockSpec(shape, lambda i, j_ref: (0,) * len(shape), pipeline_mode=pl.Buffered(1))

    return call(
        lambda *refs: second_kernel(samples, refs),
        (
            jax.ShapeDtypeStruct(pp_shape, BF16),
            jax.ShapeDtypeStruct(sec_shape, F32),
            jax.ShapeDtypeStruct(fc_shape, BF16),
            jax.ShapeDtypeStruct((2 * samples, units), F32),
        ),
        17.0,
        grid_spec=pltpu.PrefetchScalarGridSpec(
            num_scalar_prefetch=1,
            grid=(1,),
            in_specs=[const(p.shape) for p in pds] + [const(lo.shape), const(hi.shape), const(w2.shape),
                      pl.BlockSpec((channels, 1, cells, units), lambda i, j_ref: (0, j_ref[0], 0, 0), pipeline_mode=pl.Buffered(1)),
                      const(targets.shape)],
            out_specs=(const(pp_shape), const(sec_shape), const(fc_shape), const((2 * samples, units))),
            scratch_shapes=[
                pltpu.VMEM((nxb * (ny // 2) * (nz // 2) * inner, LANES), F32),
                pltpu.VMEM((channels * samples, LANES), F32),
            ],
        ),
        name="second_conv",
    )(j, *pds, lo, hi, w2, dense4, targets)


def dense_kernel(samples, own, targets_n, j_ref, hp_ref, do_ref, d_ref, sec_ref,
                 pred_ref, bh_ref, gdo_ref, bs_ref, bfc, bf):
    nxb, ny, nz, inner, _ = sec_ref.shape
    channels = d_ref.shape[0]
    cells = d_ref.shape[2]
    both = hp_ref[0]
    for t in range(1, hp_ref.shape[0]):
        both = both + hp_ref[t]
    hp = both[0:samples]
    goals = both[samples:]
    hidden = leaky_relu(hp).astype(BF16).astype(F32)
    row = lax.broadcasted_iota(jnp.int32, (samples, 1), 0)
    mine = (row // own) == j_ref[0]
    lane = lax.broadcasted_iota(jnp.int32, (samples, LANES), 1)
    preds = jnp.zeros((samples, LANES), F32)
    gdo_ref[...] = jnp.zeros_like(gdo_ref)
    back = jnp.zeros_like(hp)
    for t in range(targets_n):
        weight = do_ref[t : t + 1, :]
        pred = jnp.sum(hidden * weight, axis=1, keepdims=True)
        misfit = pred - goals[:, t : t + 1]
        preds = jnp.where(lane == t, pred, preds)
        gdo_ref[t : t + 1, :] = jnp.sum(jnp.where(mine, hidden * misfit, 0.0), axis=0, keepdims=True)
        back = back + misfit * weight
    for q in range(own):
        picked = jnp.where(row == j_ref[0] * own + q, preds, 0.0)
        pred_ref[q : q + 1, :] = jnp.sum(picked, axis=0, keepdims=True)[:, :targets_n]
    bh = (back * slope_of(hp)).astype(BF16)
    bh_ref[...] = bh

    def features(t, carry):
        for u in range(8):
            ch = t * 8 + u
            out = dot_lanes(bh, d_ref[ch, 0])
            bfc[pl.ds(pl.multiple_of(ch * samples, samples), samples), 0:cells] = out
        return carry

    lax.fori_loop(0, channels // 8, features, 0)
    half = ny // 2
    per_half = half * (nz // 2)

    def turn(s, carry):
        turned = bfc[pl.ds(s, channels, stride=samples), 0:cells].T
        for xb in range(nxb):
            for h in range(HALVES):
                start = xb * per_half * inner + h * samples + s
                at = (xb * HALVES + h) * per_half
                bf[pl.ds(start, per_half, stride=inner), :] = turned[at : at + per_half]
        return carry

    lax.fori_loop(0, samples, turn, 0)
    count = nz // 2 * inner

    def spread(t, carry):
        xb = t // half
        y3 = t % half
        start = pl.multiple_of(t * count, count)
        g = bf[pl.ds(start, count), :].reshape(nz // 2, 1, inner, LANES) * 0.125
        g = jnp.broadcast_to(g, (nz // 2, 2, inner, LANES)).reshape(nz, inner, LANES)
        for dy in range(2):
            y = 2 * y3 + dy
            slope = slope_of(sec_ref[xb, y])
            for px in range(2):
                bs_ref[2 * xb + px, y] = (g * slope[:, :, px * LANES : (px + 1) * LANES]).astype(BF16)
        return carry

    lax.fori_loop(0, nxb * half, spread, 0)


def dense_layers(j, hp, dense_out_t, dense4, sec, own):
    nxb, ny, nz, inner, _ = sec.shape
    channels, _, cells, units = dense4.shape
    samples = hp.shape[1] // 2
    targets_n = dense_out_t.shape[0]
    bs_shape = (2 * nxb, ny, nz, inner, LANES)

    def const(shape):
        return pl.BlockSpec(shape, lambda i, j_ref: (0,) * len(shape), pipeline_mode=pl.Buffered(1))

    return call(
        lambda *refs: dense_kernel(samples, own, targets_n, *refs),
        (
            jax.ShapeDtypeStruct((own, targets_n), F32),
            jax.ShapeDtypeStruct((samples, units), BF16),
            jax.ShapeDtypeStruct((8, units), F32),
            jax.ShapeDtypeStruct(bs_shape, BF16),
        ),
        11.0,
        grid_spec=pltpu.PrefetchScalarGridSpec(
            num_scalar_prefetch=1,
            grid=(1,),
            in_specs=[const(hp.shape), const(dense_out_t.shape),
                      pl.BlockSpec((channels, 1, cells, units), lambda i, j_ref: (0, j_ref[0], 0, 0), pipeline_mode=pl.Buffered(1)),
                      const(sec.shape)],
            out_specs=(const((own, targets_n)), const((samples, units)), const((8, units)), const(bs_shape)),
            scratch_shapes=[
                pltpu.VMEM((channels * samples, LANES), F32),
                pltpu.VMEM((nxb * (ny // 2) * (nz // 2) * inner, LANES), F32),
            ],
        ),
        name="dense_layers",
    )(j, hp, dense_out_t, dense4, sec)


def collect_kernel(spaces, samples, at_bh, at_grad, r_ref, t_ref, o_ref):
    everyone = r_ref.shape[0]
    groups = everyone // spaces
    chans, _, cells, _ = o_ref.shape
    total = r_ref[0, at_grad:].astype(F32)
    for t in range(1, everyone):
        total = total + r_ref[t, at_grad:].astype(F32)
    total = total.astype(BF16)
    for t in range(everyone):
        t_ref[t] = total

    def stack(j, row):
        rows = [
            r_ref[g * spaces + j, row : row + samples].astype(F32) for g in range(groups)
        ]
        return jnp.concatenate(rows, axis=0).astype(BF16)

    b = stack(0, at_bh)
    for ch in range(chans):
        for j in range(spaces):
            o_ref[ch, j] = dot_rows(stack(j, ch * samples)[:, 0:cells], b)


def collect(received, spaces, fc_shape):
    everyone = received.shape[0]
    channels, samples, cells = fc_shape
    at_bh, at_grad, end = message_rows(everyone, fc_shape)
    return call(
        lambda *refs: collect_kernel(spaces, samples, at_bh, at_grad, *refs),
        (
            jax.ShapeDtypeStruct((everyone, end - at_grad, LANES), BF16),
            jax.ShapeDtypeStruct((channels // everyone, spaces, cells, LANES), F32),
        ),
        4.0,
        name="collect",
    )(received)


def second_grad_kernel(bs_ref, pp_ref, fc_ref, bh_ref, m_ref, acc, flat):
    planes, ny, nz, inner, _ = bs_ref.shape
    nxb = planes // 2
    half = ny // 2
    rows = 2 * nz * inner
    acc[...] = jnp.zeros_like(acc)

    def step(t, carry):
        xb = t // half
        y = 2 * (t % half)
        left = jnp.concatenate(
            [bs_ref[2 * xb + px, pl.ds(y, 2)].reshape(rows, LANES) for px in range(2)], axis=1
        ).T
        for dy in range(3):
            for dz in range(3):
                right = jnp.concatenate(
                    [
                        pp_ref[xb + kk, pl.ds(y + dy, 2), dz : dz + nz].reshape(rows, LANES)
                        for kk in range(2)
                    ],
                    axis=1,
                )
                acc[dy * 3 + dz] = acc[dy * 3 + dz] + dot(left, right)
        return carry

    lax.fori_loop(0, nxb * half, step, 0)
    mid = LANES // 2
    for o in range(9):
        both = acc[o, :LANES, 0 : 3 * mid] + acc[o, LANES:, mid : 4 * mid]
        for a in range(3):
            at = a * 9 + o
            block = at // 2 * LANES
            half_at = (at % 2) * mid
            flat[block : block + LANES, half_at : half_at + mid] = both[:, a * mid : (a + 1) * mid]
    flat[13 * LANES :, mid:] = jnp.zeros((LANES, mid), F32)
    everyone = m_ref.shape[0]
    chans = fc_ref.shape[0] // everyone
    samples, cells = fc_ref.shape[1:]
    at_bh, at_grad, _ = message_rows(everyone, fc_ref.shape)
    piece = 14 * LANES // everyone
    bh = bh_ref[...].astype(F32)
    pad = jnp.zeros((at_grad - at_bh - samples, LANES), F32)
    side = jnp.concatenate([bh, pad], axis=0).astype(BF16)
    for t in range(everyone):
        f = fc_ref[t * chans : (t + 1) * chans].astype(F32).reshape(chans * samples, cells)
        m_ref[t, 0 : chans * samples, 0:cells] = f.astype(BF16)
        m_ref[t, at_bh:at_grad] = side
        m_ref[t, at_grad : at_grad + piece] = flat[t * piece : (t + 1) * piece].astype(BF16)


def message_rows(everyone, fc_shape):
    at_bh = -(-(fc_shape[0] // everyone * fc_shape[1]) // 16) * 16
    at_grad = at_bh + -(-fc_shape[1] // 16) * 16
    return at_bh, at_grad, at_grad + 14 * LANES // everyone


def second_grad(bs, pp, fc, bh, everyone):
    rows = message_rows(everyone, fc.shape)[2]
    return call(
        second_grad_kernel,
        jax.ShapeDtypeStruct((everyone, rows, LANES), BF16),
        12.0,
        scratch_shapes=[
            pltpu.VMEM((9, 2 * LANES, 2 * LANES), F32),
            pltpu.VMEM((14 * LANES, LANES), F32),
        ],
        name="second_grad",
    )(bs, pp, fc, bh)


def second_back_kernel(bs_ref, lo_ref, hi_ref, w_ref, bp_ref, pad):
    planes, ny, nz, inner, _ = bs_ref.shape
    nxb = planes // 2
    zero = jnp.zeros((inner, LANES), BF16)
    for p in range(planes + 2):

        def fill(y, carry, p=p):
            if p == 0:
                v = lo_ref[y]
            elif p == planes + 1:
                v = hi_ref[y]
            else:
                v = bs_ref[p - 1, y]
            pad[p, y + 1, 1 : nz + 1] = v
            return carry

        lax.fori_loop(0, ny, fill, 0)
        before, after = half_pads(
            pad[p, ny, 1 : nz + 1].astype(F32), pad[p, 1, 1 : nz + 1].astype(F32)
        )
        pad[p, 0, 1 : nz + 1] = before.astype(BF16)
        pad[p, ny + 1, 1 : nz + 1] = after.astype(BF16)

        def zero_ends(y, carry, p=p):
            pad[p, y, 0] = zero
            pad[p, y, nz + 1] = zero
            return carry

        lax.fori_loop(0, ny + 2, zero_ends, 0)

    quarter = ny // 4
    rows = nz * inner
    depth = 16 * LANES

    def step(t, carry):
        xb = t // quarter
        y = 4 * (t % quarter)
        out = jnp.zeros((2 * rows, 2 * LANES), F32)
        for dz in range(3):
            pieces = []
            for jx in range(4):
                for jy in range(4):
                    pieces.append(
                        jnp.concatenate(
                            [
                                pad[2 * xb + jx, y + 2 * u + jy, dz : dz + nz].reshape(rows, LANES)
                                for u in range(2)
                            ],
                            axis=0,
                        )
                    )
            sides = []
            for px in range(2):
                blocks = [
                    w_ref[dz, jx - px].reshape(depth // 4, LANES)
                    if 0 <= jx - px <= 2
                    else jnp.zeros((depth // 4, LANES), BF16)
                    for jx in range(4)
                ]
                sides.append(jnp.concatenate(blocks, axis=0))
            out = out + dot(jnp.concatenate(pieces, axis=1), jnp.concatenate(sides, axis=1))
        out = out.astype(BF16).astype(F32)
        mask = low_half((2 * rows, LANES))
        for px in range(2):
            v = out[:, px * LANES : (px + 1) * LANES]
            r = roll_half(v)
            for py in range(2):
                d = jnp.where(mask, v, r) if py == 0 else jnp.where(mask, r, v)
                d = d.astype(BF16).reshape(2, nz, inner, LANES)
                for u in range(2):
                    bp_ref[2 * xb + px, y + 2 * u + py] = d[u]
        return carry

    lax.fori_loop(0, nxb * quarter, step, 0)


def second_back(bs, lo, hi, w3):
    planes, ny, nz, inner, _ = bs.shape
    return call(
        second_back_kernel,
        jax.ShapeDtypeStruct(bs.shape, BF16),
        12.0,
        scratch_shapes=[pltpu.VMEM((planes + 2, ny + 2, nz + 2, inner, LANES), BF16)],
        name="second_back",
    )(bs, lo, hi, w3)


def active_of(f, bp, mean, inverse, gain, shift):
    nz, inner, _ = f.shape
    w = (f.reshape(nz * inner, 2 * LANES) - mean) * inverse
    slope = slope_of(gain * w + shift)
    g = bp.astype(F32).reshape(nz // 2, 1, inner, LANES) * 0.125
    g = jnp.broadcast_to(g, (nz // 2, 2, inner, LANES)).reshape(nz * inner, LANES)
    return w, slope * jnp.concatenate([g, g], axis=1)


def sums_kernel(local_count, total_count, f_ref, bp_ref, st_ref, gs_ref, o_ref, acc):
    i = pl.program_id(0)
    mean, inverse = group_stats(st_ref[...], local_count, total_count)
    mean, inverse = wide(mean), wide(inverse)
    gain, shift = wide(gs_ref[0:1]), wide(gs_ref[1:2])

    @pl.when(i == 0)
    def _():
        acc[...] = jnp.zeros_like(acc)

    def step(yb, carry):
        w, active = active_of(f_ref[0, yb], bp_ref[0, yb], mean, inverse, gain, shift)
        acc[0] = acc[0] + jnp.sum((active * w).reshape(-1, 8, 2 * LANES), axis=0)
        acc[1] = acc[1] + jnp.sum(active.reshape(-1, 8, 2 * LANES), axis=0)
        return carry

    lax.fori_loop(0, f_ref.shape[1], step, 0)

    @pl.when(i == pl.num_programs(0) - 1)
    def _():
        rows = [jnp.sum(acc[k], axis=0, keepdims=True) for k in range(2)]
        rows = [both_halves(r[:, :LANES] + r[:, LANES:]) for r in rows]
        o_ref[...] = jnp.concatenate(rows, axis=0)


def norm_sums(f, bp, st, gs, local_count, total_count):
    return call(
        lambda *refs: sums_kernel(local_count, total_count, *refs),
        jax.ShapeDtypeStruct((2, LANES), F32),
        13.0,
        grid=(f.shape[0],),
        in_specs=[
            pl.BlockSpec((1,) + f.shape[1:], lambda i: (i, 0, 0, 0, 0)),
            pl.BlockSpec((1,) + bp.shape[1:], lambda i: (i, 0, 0, 0, 0)),
            whole_spec(st.shape),
            whole_spec(gs.shape),
        ],
        out_specs=whole_spec((2, LANES)),
        scratch_shapes=[pltpu.VMEM((2, 8, 2 * LANES), F32)],
        name="norm_sums",
    )(f, bp, st, gs)


def first_grad_kernel(local_count, total_count, c, f_ref, bp_ref, st_ref, gs_ref, sum_ref, own_ref, gdo_ref, xa_ref, xc_ref, g_ref, acc):
    i = pl.program_id(0)
    mean, inverse = group_stats(st_ref[...], local_count, total_count)
    mean, inverse = wide(mean), wide(inverse)
    gain, shift = wide(gs_ref[0:1]), wide(gs_ref[1:2])
    group_sums = jnp.sum(sum_ref[...], axis=0)
    cross = wide(group_sums[0:1]) * (1.0 / total_count)
    plain = wide(group_sums[1:2]) * (1.0 / total_count)
    scale = gain * inverse
    nz = f_ref.shape[2]
    inner = f_ref.shape[3]
    rows = nz * inner

    @pl.when(i == 0)
    def _():
        acc[...] = jnp.zeros_like(acc)

    def step(yb, carry):
        w, active = active_of(f_ref[0, yb], bp_ref[0, yb], mean, inverse, gain, shift)
        left = (scale * (active - plain - w * cross)).astype(BF16).T
        for dz in range(3):
            for kk, x_ref in enumerate((xa_ref, xc_ref)):
                right = jnp.concatenate(
                    [x_ref[0, yb + mm, dz : dz + nz].reshape(rows, LANES) for mm in range(2)],
                    axis=1,
                )
                acc[dz * 2 + kk] = acc[dz * 2 + kk] + dot(left, right)
        return carry

    lax.fori_loop(0, f_ref.shape[1], step, 0)

    @pl.when(i == pl.num_programs(0) - 1)
    def _():
        co = LANES // 2
        blocks = -(-27 * c // LANES)
        g_ref[(blocks - 1) * co :, :] = jnp.zeros((g_ref.shape[0] - (blocks - 1) * co, LANES), F32)
        g_ref[blocks * co : blocks * co + 2, :] = own_ref[...]
        g_ref[blocks * co + 8 : blocks * co + 16, :] = gdo_ref[...]
        for a in range(3):
            for b in range(3):
                for d in range(3):
                    total = None
                    for px in range(2):
                        for py in range(2):
                            xw, yw = a + px, b + py
                            at = (yw // 2) * LANES + (yw % 2) * 2 * c + (xw % 2) * c
                            top = (px * 2 + py) * co
                            part = acc[d * 2 + xw // 2, top : top + co, at : at + c]
                            total = part if total is None else total + part
                    at = ((a * 3 + b) * 3 + d) * c
                    row = at // LANES * co
                    g_ref[row : row + co, at % LANES : at % LANES + c] = total


def first_grad(f, bp, st, gs, sums, own, gdo, xb, c, local_count, total_count, rows):
    x_block = (1,) + xb.shape[1:]
    out = (rows, LANES)
    return call(
        lambda *refs: first_grad_kernel(local_count, total_count, c, *refs),
        jax.ShapeDtypeStruct(out, F32),
        33.0,
        grid=(f.shape[0],),
        in_specs=[
            pl.BlockSpec((1,) + f.shape[1:], lambda i: (i, 0, 0, 0, 0)),
            pl.BlockSpec((1,) + bp.shape[1:], lambda i: (i, 0, 0, 0, 0)),
            whole_spec(st.shape),
            whole_spec(gs.shape),
            whole_spec(sums.shape),
            whole_spec(own.shape),
            whole_spec(gdo.shape),
            pl.BlockSpec(x_block, lambda i: (i, 0, 0, 0, 0)),
            pl.BlockSpec(x_block, lambda i: (i + 1, 0, 0, 0, 0)),
        ],
        out_specs=whole_spec(out),
        scratch_shapes=[pltpu.VMEM((6, 2 * LANES, 2 * LANES), F32)],
        name="first_grad",
    )(f, bp, st, gs, sums, own, gdo, xb, xb)


def add_kernel(r_ref, o_ref):
    total = r_ref[0]
    for t in range(1, r_ref.shape[0]):
        total = total + r_ref[t]
    total = total.astype(BF16)
    for t in range(o_ref.shape[0]):
        o_ref[t] = total


def add_parts(parts):
    return call(add_kernel, jax.ShapeDtypeStruct(parts.shape, BF16), 2.0, name="add_parts")(parts)


def gather_all(value, axis):
    count = lax.axis_size(axis)
    others = [
        lax.ppermute(value, axis, [(i, (i + k) % count) for i in range(count)])
        for k in range(1, count)
    ]
    return jnp.stack([value] + others)


def swap(parts, axes):
    return lax.all_to_all(parts, axes, split_axis=0, concat_axis=0, tiled=True)


def finish_second_kernel(r_ref, g_ref):
    columns = g_ref.shape[1]
    for k in range(r_ref.shape[0]):
        width = min(LANES, columns - k * LANES)
        g_ref[:, k * LANES : k * LANES + width] = r_ref[k].astype(F32)[:, 0:width]


def finish_first_kernel(r_ref, g_ref, n_ref, gdo_ref):
    co, columns = g_ref.shape
    blocks = -(-columns // LANES)
    for k in range(blocks):
        width = min(LANES, columns - k * LANES)
        g_ref[:, k * LANES : k * LANES + width] = r_ref[k * co : (k + 1) * co].astype(F32)[:, 0:width]
    tail = r_ref[blocks * co : blocks * co + 16].astype(F32)
    n_ref[...] = tail[0:2, 0 : n_ref.shape[1]]
    gdo_ref[...] = tail[8:16].T[:, 0 : gdo_ref.shape[1]]


def swap_edges(first, last, axis):
    count = lax.axis_size(axis)
    before = lax.ppermute(last, axis, [(i, i + 1) for i in range(count - 1)])
    after = lax.ppermute(first, axis, [(i + 1, i) for i in range(count - 1)])
    return before, after


def shards(inputs, conv_in, norm_gain, norm_shift, conv_out, dense_in, dense_out, targets):
    samples, c, planes, cells = inputs.shape
    spaces = lax.axis_size("space")
    groups = lax.axis_size("dp")
    units = dense_in.shape[1]
    channels = conv_out.shape[0]
    own = targets.shape[0]
    local_count = float(samples * planes * cells)
    total_count = local_count * spaces

    everyone = groups * spaces
    world = ("dp", "space")

    before, after = swap_edges(inputs[:, :, :1], inputs[:, :, planes - 1 :], "space")
    w1, w2, v3 = make_weights(conv_in, conv_out)
    xi = prepare(inputs.reshape(samples, c * planes, cells), planes, c)
    gs = jnp.stack([norm_gain, norm_shift])
    gs = jnp.concatenate([gs, gs], axis=1)
    j = lax.axis_index("space").astype(jnp.int32).reshape(1)
    dense4 = dense_in.reshape(channels, spaces, dense_in.shape[0] // (channels * spaces), units)
    halo = jnp.concatenate([before, after], axis=1).reshape(samples, 2 * c, cells)

    f, xb, st = first_conv(xi, halo, w1, planes)
    stats = gather_all(st, "space")
    outer, edge = normalise_pool(f, stats, gs, local_count, total_count, True)
    lo, hi = swap_edges(edge[0], edge[1], "space")
    pds = [outer]
    if planes > 4:
        pds += normalise_pool(f, stats, gs, local_count, total_count, False)
    pp, sec, fc, partial = second_conv(j, pds, lo, hi, w2, dense4, targets, samples)
    hp = gather_all(partial, "space")
    predictions, bh, gdo, bs = dense_layers(j, hp, dense_out.astype(F32).T, dense4, sec, own)
    bs_lo, bs_hi = swap_edges(bs[0], bs[-1], "space")
    message = second_grad(bs, pp, fc, bh, everyone)
    received = swap(message, world)
    bp = second_back(bs, bs_lo, bs_hi, v3)
    own_sums = norm_sums(f, bp, stats, gs, local_count, total_count)
    sums = gather_all(own_sums, "space")
    totals, grad_dense_in = collect(received, spaces, fc.shape)
    totals = swap(totals, world)
    used = -(-conv_in.shape[1] // LANES) * conv_in.shape[0] + 16
    rows = -(-used // everyone)
    rows = (-(-rows // 8) * 8 if rows > 8 else rows) * everyone
    local_in = first_grad(
        f, bp, stats, gs, sums, own_sums, gdo, xb, c, local_count, total_count, rows
    )
    parts = swap(local_in.reshape(everyone, -1, LANES), world)
    grad_conv_out = call(
        finish_second_kernel,
        jax.ShapeDtypeStruct(conv_out.shape, F32),
        2.0,
        name="finish_second",
    )(totals.reshape(14, LANES, LANES))
    sent = add_parts(parts)
    totals = swap(sent, world)
    grad_conv_in, grad_norm, grad_dense_out = call(
        finish_first_kernel,
        (
            jax.ShapeDtypeStruct(conv_in.shape, F32),
            jax.ShapeDtypeStruct((2, norm_gain.shape[0]), F32),
            jax.ShapeDtypeStruct(dense_out.shape, F32),
        ),
        name="finish_first",
    )(totals.reshape(rows, LANES))
    return (
        grad_conv_in,
        grad_norm,
        grad_conv_out,
        grad_dense_in.reshape(-1, units),
        grad_dense_out,
        predictions,
    )


def solution(mesh):
    placed = (P("dp", None, "space", None), P(), P(), P(), P(), P(), P(), P(("dp", "space"), None))
    return jax.shard_map(
        shards,
        mesh=mesh,
        in_specs=placed,
        out_specs=(P(), P(), P(), P(("dp", "space"), None), P(), P(("dp", "space"), None)),
        check_vma=False,
    )
```

```python
import jax
import jax.numpy as jnp
import numpy as np
from jax import lax
from jax.experimental import pallas as pl
from jax.experimental.pallas import tpu as pltpu
from jax.sharding import PartitionSpec as P


GRID = 32
HALVES = 2
LANES = 128
norm_epsilon = 1e-05
INTERPRET = False

F32 = jnp.float32
BF16 = jnp.bfloat16


def leaky_relu(values):
    return values * (0.65 + 0.35 * jnp.tanh(values))


def slope_of(values):
    bent = jnp.tanh(values)
    return 0.65 + 0.35 * (bent + values * (1.0 - bent * bent))


def dot(a, b):
    return jnp.dot(a, b, preferred_element_type=F32)


def dot_rows(a, b):
    return lax.dot_general(a, b, (((0,), (0,)), ((), ())), preferred_element_type=F32)


def dot_lanes(a, b):
    return lax.dot_general(a, b, (((1,), (1,)), ((), ())), preferred_element_type=F32)


def low_half(shape):
    return lax.broadcasted_iota(jnp.int32, shape, len(shape) - 1) < LANES // 2


def roll_half(values):
    flat = values.reshape(-1, LANES)
    return pltpu.roll(flat, LANES // 2, 1).reshape(values.shape)


def both_halves(values):
    return values + roll_half(values)


def call(kernel, out_shape, cost_us=1.0, **kwargs):
    cost = pl.CostEstimate(
        flops=int(cost_us * 1e9), bytes_accessed=int(cost_us * 3e6), transcendentals=0
    )
    return pl.pallas_call(
        kernel, out_shape=out_shape, interpret=INTERPRET, cost_estimate=cost, **kwargs
    )


def whole_spec(shape):
    return pl.BlockSpec(shape, lambda *_: (0,) * len(shape), pipeline_mode=pl.Buffered(1))


def offset(a, b, d):
    return (a * 3 + b) * 3 + d


def first_weights_kernel(c_in, ci_ref, w1_ref, t0, t1):
    t0[...] = jnp.zeros_like(t0)
    t0[0 : ci_ref.shape[0], 0 : ci_ref.shape[1]] = ci_ref[...].astype(F32)
    for k in range(t0.shape[1] // LANES):
        lanes = slice(k * LANES, (k + 1) * LANES)
        t1[lanes, :] = both_halves(t0[:, lanes].T)
    mask = low_half((c_in, LANES))
    zero = jnp.zeros((c_in, LANES), F32)
    row = 0
    for d in range(3):
        for kk in range(2):
            for mm in range(2):
                for yo in range(2):
                    for xo in range(2):
                        for px in range(2):
                            a = 2 * kk + xo - px
                            parts = []
                            for py in range(2):
                                b = 2 * mm + yo - py
                                if 0 <= a <= 2 and 0 <= b <= 2:
                                    at = offset(a, b, d) * c_in
                                    parts.append(t1[at : at + c_in, :])
                                else:
                                    parts.append(zero)
                            w1_ref[row : row + c_in, px * LANES : (px + 1) * LANES] = jnp.where(
                                mask, parts[0], parts[1]
                            ).astype(BF16)
                        row += c_in


def second_weights_kernel(c_mid, co_ref, w2_ref, v3_ref, t0, t2):
    columns = co_ref.shape[0]
    t2[0:columns] = co_ref[...].astype(F32)
    t2[columns:] = jnp.zeros((t2.shape[0] - columns, LANES), F32)
    for k in range(t0.shape[1] // LANES):
        lanes = slice(k * LANES, (k + 1) * LANES)
        t0[:, lanes] = t2[lanes, :].T
    row = 0
    for b in range(3):
        for d in range(3):
            for xw in range(4):
                for px in range(2):
                    a = xw - px
                    if 0 <= a <= 2:
                        at = offset(a, b, d) * c_mid
                        part = t2[at : at + c_mid, :].astype(BF16)
                    else:
                        part = jnp.zeros((c_mid, LANES), BF16)
                    w2_ref[row : row + c_mid, px * LANES : (px + 1) * LANES] = part
                row += c_mid
    mask = low_half((LANES, LANES))
    zero = jnp.zeros((LANES, LANES), F32)
    for d in range(3):
        for a in range(3):
            for yw in range(4):
                parts = []
                for py in range(2):
                    b = yw - py
                    if 0 <= b <= 2:
                        o = offset(2 - a, 2 - b, 2 - d)
                        v = t0[:, o // 2 * LANES : (o // 2 + 1) * LANES]
                        parts.append(v if o % 2 == py else roll_half(v))
                    else:
                        parts.append(zero)
                v3_ref[d, a, yw] = jnp.where(mask, parts[0], parts[1]).astype(BF16)


def first_weights(conv_in):
    c_in = conv_in.shape[1] // 27
    width = -(-conv_in.shape[1] // LANES) * LANES
    return call(
        lambda *refs: first_weights_kernel(c_in, *refs),
        jax.ShapeDtypeStruct((48 * c_in, 2 * LANES), BF16),
        2.0,
        scratch_shapes=[pltpu.VMEM((LANES, width), F32), pltpu.VMEM((width, LANES), F32)],
        name="first_weights",
    )(conv_in)


def second_weights(conv_out):
    c_mid = conv_out.shape[1] // 27
    width = -(-conv_out.shape[1] // LANES) * LANES
    return call(
        lambda *refs: second_weights_kernel(c_mid, *refs),
        (
            jax.ShapeDtypeStruct((36 * c_mid, 2 * LANES), BF16),
            jax.ShapeDtypeStruct((3, 3, 4, LANES, LANES), BF16),
        ),
        3.0,
        scratch_shapes=[pltpu.VMEM((LANES, width), F32), pltpu.VMEM((width, LANES), F32)],
        name="second_weights",
    )(conv_out.T)


def half_pads(before, after):
    zero = jnp.zeros_like(before[:, 0:8])
    return (
        jnp.concatenate([zero, before[:, 0:8]], axis=1),
        jnp.concatenate([after[:, 8:16], zero], axis=1),
    )


def split_sample(read, sel_ref, ub_ref, s, samples):
    half_y = GRID // HALVES
    last = half_y // 2
    width = ub_ref.shape[3]
    half = LANES // 2
    per_group = LANES // GRID

    def put(h, m, part, value):
        for k in range(width // LANES):
            at = k * LANES + part * half
            ub_ref[h * samples + s, m, :, at : at + half] = value[:, at : at + half]

    for g in range(GRID * GRID // LANES):
        val = dot_rows(read(slice(g * LANES, (g + 1) * LANES)), sel_ref[...]).astype(BF16)
        for r in range(per_group):
            y = g * per_group + r
            h, local = y // half_y, y % half_y
            v = val[r * GRID : (r + 1) * GRID]
            if y % 2:
                put(h, (local + 1) // 2, 0, v)
                if local == half_y - 1 and h + 1 < HALVES:
                    put(h + 1, 0, 0, v)
            else:
                put(h, local // 2, 1, v)
                if local == 0 and h > 0:
                    put(h - 1, last, 1, v)
    zero = jnp.zeros((GRID, width), BF16)
    put(0, 0, 0, zero)
    put(HALVES - 1, last, 1, zero)


def weave(ub_ref, perm_ref, m, part):
    slots = ub_ref.shape[0]
    rows = jnp.concatenate(
        [ub_ref[t, m, part * slots : (part + 1) * slots, :] for t in range(slots)], axis=0
    )
    return dot(perm_ref[...], rows).astype(BF16)


def weave_matrix(slots):
    perm = np.zeros((slots * slots, slots * slots), np.float32)
    for z in range(slots):
        for t in range(slots):
            perm[z * slots + t, t * slots + z] = 1.0
    return jnp.asarray(perm, BF16)


def prepare_kernel(steps, x_ref, pa_ref, perm_ref, xb_ref, ub_ref):
    i = pl.program_id(0)
    batch = x_ref.shape[0]
    samples = batch * steps
    inner = HALVES * samples
    per_step = xb_ref.shape[1]

    @pl.when(i < steps)
    def _():
        def split(t, carry):
            split_sample(
                lambda lanes: x_ref[t, :, lanes], pa_ref, ub_ref, i * batch + t, samples
            )
            return carry

        lax.fori_loop(0, batch, split, 0)

    @pl.when(i >= steps)
    def _():
        zero = jnp.zeros((inner, LANES), BF16)

        def join(t, carry):
            m = (i - steps) * per_step + t
            for part in range(GRID // inner):
                out = weave(ub_ref, perm_ref, m, part)
                for k in range(xb_ref.shape[0]):
                    at = 1 + part * inner
                    xb_ref[k, t, at : at + inner] = out[:, k * LANES : (k + 1) * LANES].reshape(
                        inner, inner, LANES
                    )
            for k in range(xb_ref.shape[0]):
                xb_ref[k, t, 0] = zero
                xb_ref[k, t, GRID + 1] = zero
            return carry

        lax.fori_loop(0, per_step, join, 0)


def prepare(x, planes, c):
    samples = x.shape[0]
    pairs = planes // 2 + 1
    inner = HALVES * samples
    ms = GRID // HALVES // 2 + 1
    batch, per_step = samples // 4, ms // 3
    pa = np.zeros((c * planes, pairs * LANES), np.float32)
    for ch in range(c):
        for k in range(pairs):
            for yo in range(2):
                for xo in range(2):
                    p = 2 * k - 1 + xo
                    if 0 <= p < planes:
                        pa[ch * planes + p, k * LANES + yo * 2 * c + xo * c + ch] = 1.0
    pa = jnp.asarray(pa, BF16)
    perm = weave_matrix(inner)
    block = (pairs, per_step, GRID + 2, inner, LANES)
    return call(
        lambda *refs: prepare_kernel(4, *refs),
        jax.ShapeDtypeStruct((pairs, ms, GRID + 2, inner, LANES), BF16),
        11.0,
        grid=(4 + 3,),
        in_specs=[
            pl.BlockSpec((batch,) + x.shape[1:], lambda i: (jnp.minimum(i, 3), 0, 0)),
            whole_spec(pa.shape),
            whole_spec(perm.shape),
        ],
        out_specs=pl.BlockSpec(block, lambda i: (0, jnp.maximum(i - 4, 0), 0, 0, 0)),
        scratch_shapes=[pltpu.VMEM((inner, ms, GRID, pairs * LANES), BF16)],
        name="prepare",
    )(x, pa, perm)


def edge_kernel(x_ref, sel_ref, lo_ref, hi_ref):
    c = lo_ref.shape[1]
    for t in range(x_ref.shape[0]):
        out = dot(sel_ref[...], x_ref[t]).astype(BF16)
        lo_ref[t] = out[0:c]
        hi_ref[t] = out[c:]


def edge_planes(x, planes, c):
    samples, rows, cells = x.shape
    sel = np.zeros((2 * c, rows), np.float32)
    for ch in range(c):
        sel[ch, ch * planes] = 1.0
        sel[c + ch, ch * planes + planes - 1] = 1.0
    sel = jnp.asarray(sel, BF16)
    out = jax.ShapeDtypeStruct((samples, c, cells), BF16)
    batch = samples // 2
    spec = pl.BlockSpec((batch, c, cells), lambda i: (i, 0, 0))
    return call(
        edge_kernel,
        (out, out),
        2.5,
        grid=(2,),
        in_specs=[pl.BlockSpec((batch, rows, cells), lambda i: (i, 0, 0)), whole_spec(sel.shape)],
        out_specs=(spec, spec),
        name="edge_planes",
    )(x, sel)


def first_kernel(planes, samples, refs):
    (xa_ref, xc_ref, lo_ref, hi_ref, pb_ref, perm_ref, w_ref,
     f_ref, xe_ref, st_ref, cur, ub, eb, w_acc) = refs
    i = pl.program_id(0)
    half_y = GRID // HALVES
    inner = HALVES * samples
    rows = GRID * inner
    blocks = half_y // 2
    per_block = rows // 8
    end = pl.num_programs(0) - 1

    @pl.when(i == 0)
    def _():
        def split(s, carry):
            split_sample(
                lambda lanes: jnp.concatenate([lo_ref[s, :, lanes], hi_ref[s, :, lanes]], axis=0),
                pb_ref, ub, s, samples,
            )
            return carry

        lax.fori_loop(0, samples, split, 0)

        def join(m, carry):
            for part in range(GRID // inner):
                at = part * inner
                eb[m, at : at + inner] = weave(ub, perm_ref, m, part).reshape(inner, inner, LANES)
            return carry

        lax.fori_loop(0, blocks + 1, join, 0)
        w_acc[...] = jnp.zeros_like(w_acc)

    def patched(k, x_ref):
        def body(m, carry):
            lane = lax.broadcasted_iota(jnp.int32, (rows, LANES), 1)
            halo = (lane % (LANES // 2) < LANES // 4) == (k == 0)
            own = x_ref[0, m, 1 : GRID + 1].astype(F32).reshape(rows, LANES)
            edge = eb[m].astype(F32).reshape(rows, LANES)
            both = jnp.where(halo, edge, own).astype(BF16).reshape(GRID, inner, LANES)
            zero = jnp.zeros((inner, LANES), BF16)
            for ref, at in ((cur, k), (xe_ref, k)):
                ref[at, m, 0] = zero
                ref[at, m, 1 : GRID + 1] = both
                ref[at, m, GRID + 1] = zero
            return carry

        lax.fori_loop(0, blocks + 1, body, 0)

    def copied(k, x_ref):
        def body(m, carry):
            cur[k, m] = x_ref[0, m]
            return carry

        lax.fori_loop(0, blocks + 1, body, 0)

    pl.when(i == 0)(lambda: patched(0, xa_ref))
    pl.when(i > 0)(lambda: copied(0, xa_ref))
    pl.when(i == end)(lambda: patched(1, xc_ref))
    pl.when(i < end)(lambda: copied(1, xc_ref))

    def conv(yb):
        pieces = []
        for dz in range(3):
            for kk in range(2):
                for mm in range(2):
                    pieces.append(
                        cur[kk, yb + mm, dz : dz + GRID].reshape(rows, LANES)
                    )
        out = dot(jnp.concatenate(pieces, axis=1), w_ref[...])
        f_ref[0, yb] = out.reshape(GRID, inner, 2 * LANES)

    def stats(yb):
        stacked = f_ref[0, yb].reshape(per_block, 8, 2 * LANES)
        mean = jnp.sum(stacked, axis=0) * (1.0 / per_block)
        dev = stacked - mean[None]
        square = jnp.sum(dev * dev, axis=0)
        done = (i * blocks + yb).astype(F32)
        delta = mean - w_acc[0]
        w_acc[0] = w_acc[0] + delta / (done + 1.0)
        w_acc[1] = w_acc[1] + square + delta * delta * (per_block * done / (done + 1.0))

    def step(yb, carry):
        stats(yb - 1)
        conv(yb)
        return carry

    conv(0)
    lax.fori_loop(1, blocks, step, 0)
    stats(blocks - 1)

    @pl.when(i == pl.num_programs(0) - 1)
    def _():
        count = float(per_block * blocks * (planes // 2))
        mean = w_acc[0]
        m = jnp.mean(mean, axis=0, keepdims=True)
        m = both_halves((m[:, :LANES] + m[:, LANES:]) * 0.5) * 0.5
        dev = mean - wide(m)
        q = jnp.sum(w_acc[1] + count * dev * dev, axis=0, keepdims=True)
        q = both_halves(q[:, :LANES] + q[:, LANES:])
        st = jnp.concatenate([m, q], axis=0)
        st_ref[...] = st


def first_conv(xi, lo, hi, w1, planes):
    samples, c, _ = lo.shape
    inner = HALVES * samples
    half_y = GRID // HALVES
    pb = np.zeros((2 * c, LANES), np.float32)
    for ch in range(2 * c):
        pb[ch, ch] = 1.0
        pb[ch, LANES // 2 + ch] = 1.0
    pb = jnp.asarray(pb, BF16)
    perm = weave_matrix(inner)
    nxb = planes // 2
    f_shape = (nxb, half_y // 2, GRID, inner, 2 * LANES)
    x_block = (1,) + xi.shape[1:]
    xe_shape = (2,) + xi.shape[1:]
    return call(
        lambda *refs: first_kernel(planes, samples, refs),
        (
            jax.ShapeDtypeStruct(f_shape, F32),
            jax.ShapeDtypeStruct(xe_shape, BF16),
            jax.ShapeDtypeStruct((2, LANES), F32),
        ),
        25.0,
        grid=(nxb,),
        in_specs=[
            pl.BlockSpec(x_block, lambda i: (i, 0, 0, 0, 0)),
            pl.BlockSpec(x_block, lambda i: (i + 1, 0, 0, 0, 0)),
        ] + [whole_spec(a.shape) for a in (lo, hi, pb, perm, w1)],
        out_specs=(
            pl.BlockSpec((1,) + f_shape[1:], lambda i: (i, 0, 0, 0, 0)),
            whole_spec(xe_shape),
            whole_spec((2, LANES)),
        ),
        scratch_shapes=[
            pltpu.VMEM(xe_shape, BF16),
            pltpu.VMEM((inner, half_y // 2 + 1, GRID, LANES), BF16),
            pltpu.VMEM((half_y // 2 + 1, GRID, inner, LANES), BF16),
            pltpu.VMEM((2, 8, 2 * LANES), F32),
        ],
        name="first_conv",
    )(xi, xi, lo, hi, pb, perm, w1)


def group_stats(refs, local_count, total_count):
    count = len(refs)
    mean = sum(ref[0:1] for ref in refs) * (1.0 / count)
    square = sum(ref[1:2] for ref in refs)
    for ref in refs:
        dev = ref[0:1] - mean
        square = square + local_count * dev * dev
    inverse = lax.rsqrt(square / total_count + norm_epsilon)
    return mean, inverse


def wide(row):
    return jnp.concatenate([row, row], axis=1)


def pool_kernel(local_count, total_count, count, refs):
    f_ref, gs_ref, *st_refs = refs[: count + 2]
    pd_ref, *edge_refs = refs[count + 2 :]
    mean, inverse = group_stats(st_refs, local_count, total_count)
    scale = gs_ref[0:1] * inverse
    mean, scale, shift = wide(mean), wide(scale), wide(gs_ref[1:2])
    nyb = f_ref.shape[1]
    nz = f_ref.shape[2]
    inner = f_ref.shape[3]

    size = 4

    def step(yb, carry):
        for z in range(0, nz, size):
            f = f_ref[0, yb, z : z + size].reshape(size * inner, 2 * LANES)
            act = leaky_relu((f - mean) * scale + shift)
            act = act[:, :LANES] + act[:, LANES:]
            act = act.reshape(size // 2, 2, inner, LANES)
            act = act[:, 0] + act[:, 1]
            pooled = both_halves(act) * 0.125
            pd_ref[0, yb, z // 2 : (z + size) // 2] = pooled.astype(BF16)
        return carry

    lax.fori_loop(0, nyb, step, 0)
    half = nyb // 2

    def pack(ref):
        mask = low_half((nz // 2, inner, LANES))
        for y in range(half):
            ref[y] = jnp.where(
                mask, pd_ref[0, y].astype(F32), pd_ref[0, y + half].astype(F32)
            ).astype(BF16)

    for t, ref in enumerate(edge_refs):
        pl.when(pl.program_id(0) == t)(lambda ref=ref: pack(ref))


def normalise_pool(f, stats, gs, local_count, total_count, edges):
    nxb, nyb, nz, inner, _ = f.shape
    count = 2 if edges else nxb - 2
    stride, base = (nxb - 1, 0) if edges else (1, 1)
    pd_shape = (count, nyb, nz // 2, inner, LANES)
    edge = (nyb // 2, nz // 2, inner, LANES)
    shapes = [jax.ShapeDtypeStruct(pd_shape, BF16)]
    specs = [pl.BlockSpec((1,) + pd_shape[1:], lambda i: (i, 0, 0, 0, 0))]
    if edges:
        shapes += [jax.ShapeDtypeStruct(edge, BF16)] * 2
        specs += [whole_spec(edge)] * 2
    return call(
        lambda *refs: pool_kernel(local_count, total_count, len(stats), refs),
        shapes,
        3.0 * count,
        grid=(count,),
        in_specs=[
            pl.BlockSpec((1,) + f.shape[1:], lambda i: (i * stride + base, 0, 0, 0, 0)),
            whole_spec(gs.shape),
        ] + [whole_spec(st.shape) for st in stats],
        out_specs=specs,
        name="pool_edges" if edges else "pool_inside",
    )(f, gs, *stats)


def dense_copies(d_ref, j_ref, dbuf, sems):
    parts = sems.shape[0]
    size = dbuf.shape[0] // parts
    return [
        pltpu.make_async_copy(
            d_ref.at[pl.ds(p * size, size), j_ref[0]], dbuf.at[pl.ds(p * size, size)], sems.at[p]
        )
        for p in range(parts)
    ]


def second_kernel(samples, refs):
    (j_ref, pe_ref, *mid, lo_ref, hi_ref, w_ref, d_ref, tg_ref,
     pp_ref, sec_ref, fc_ref, hid_ref, ft, fcs, dbuf, sems) = refs
    copies = dense_copies(d_ref, j_ref, dbuf, sems)
    for copy in copies:
        copy.start()
    edges, ny, nz, inner, _ = pe_ref.shape
    planes = edges + (mid[0].shape[0] if mid else 0)

    def plane(p, y):
        if p == 0 or p == planes - 1:
            return pe_ref[min(p, 1), y].astype(F32)
        return mid[0][p - 1, y].astype(F32)

    pairs = planes // 2 + 1
    half = ny // 2
    cells = fc_ref.shape[2]
    channels = fc_ref.shape[0]

    def unpack(ref, y):
        v = ref[y % half].astype(F32)
        return jnp.where(low_half(v.shape) == (y < half), v, roll_half(v))

    def assemble(y, carry):
        mask = low_half((nz, inner, LANES))
        for k in range(pairs):
            a = unpack(lo_ref, y) if k == 0 else plane(2 * k - 1, y)
            b = unpack(hi_ref, y) if k == pairs - 1 else plane(2 * k, y)
            pp_ref[k, y + 1, 1 : nz + 1] = jnp.where(mask, a, b).astype(BF16)
        return carry

    lax.fori_loop(0, ny, assemble, 0)
    zero = jnp.zeros((inner, LANES), BF16)
    for k in range(pairs):
        last = pp_ref[k, ny, 1 : nz + 1].astype(F32)
        head = pp_ref[k, 1, 1 : nz + 1].astype(F32)
        before, after = half_pads(last, head)
        pp_ref[k, 0, 1 : nz + 1] = before.astype(BF16)
        pp_ref[k, ny + 1, 1 : nz + 1] = after.astype(BF16)

        def zero_ends(y, carry, k=k):
            pp_ref[k, y, 0] = zero
            pp_ref[k, y, nz + 1] = zero
            return carry

        lax.fori_loop(0, ny + 2, zero_ends, 0)

    rows = 2 * nz * inner

    def conv(t, carry):
        xb = t // half
        y3 = t % half
        y = 2 * y3
        pieces = []
        for dy in range(3):
            for dz in range(3):
                for kk in range(2):
                    pieces.append(
                        pp_ref[xb + kk, pl.ds(y + dy, 2), dz : dz + nz].reshape(rows, LANES)
                    )
        out = dot(jnp.concatenate(pieces, axis=1), w_ref[...])
        sec_ref[xb, pl.ds(y, 2)] = out.reshape(2, nz, inner, 2 * LANES)
        act = leaky_relu(out)
        act = act[:, :LANES] + act[:, LANES:]
        act = act.reshape(2, nz // 2, 2, inner, LANES)
        act = (act[0, :, 0] + act[0, :, 1]) + (act[1, :, 0] + act[1, :, 1])
        act = (act * 0.125).astype(BF16).astype(F32)
        count = nz // 2 * inner
        start = pl.multiple_of((xb * half + y3) * count, count)
        ft[pl.ds(start, count), :] = act.reshape(count, LANES)
        return carry

    nxb = planes // 2
    lax.fori_loop(0, nxb * half, conv, 0)

    per_half = half * (nz // 2)

    def turn(s, carry):
        parts = []
        for xb in range(nxb):
            for h in range(HALVES):
                start = xb * per_half * inner + h * samples + s
                parts.append(ft[pl.ds(start, per_half, stride=inner), :])
        turned = jnp.concatenate(parts, axis=0).T
        fcs[pl.ds(s, channels, stride=samples), 0:cells] = turned
        return carry

    lax.fori_loop(0, samples, turn, 0)
    fc_ref[...] = fcs[:, 0:cells].reshape(channels, samples, cells).astype(BF16)

    def dense(t, acc):
        for u in range(8):
            ch = t * 8 + u
            acc[u % 4] = acc[u % 4] + dot(fc_ref[ch], dbuf[ch])
        return acc

    zeros = [jnp.zeros((samples, LANES), F32) for _ in range(4)]
    acc = zeros
    size = channels // 8 // len(copies)
    for p, copy in enumerate(copies):
        copy.wait()
        acc = lax.fori_loop(p * size, (p + 1) * size, dense, acc)
    total = (acc[0] + acc[1]) + (acc[2] + acc[3])
    own, targets_n = tg_ref.shape
    hid_ref[0:samples] = total
    hid_ref[samples : 2 * samples] = jnp.zeros_like(total)
    for q in range(own):
        at = samples + j_ref[0] * own + q
        hid_ref[pl.ds(at, 1), 0:targets_n] = tg_ref[q : q + 1, :]


def second_conv(j, pds, lo, hi, w2, dense4, targets, samples):
    _, ny, nz, inner, _ = pds[0].shape
    planes = sum(p.shape[0] for p in pds)
    channels, _, cells, units = dense4.shape
    pairs = planes // 2 + 1
    nxb = planes // 2
    pp_shape = (pairs, ny + 2, nz + 2, inner, LANES)
    sec_shape = (nxb, ny, nz, inner, 2 * LANES)
    fc_shape = (channels, samples, cells)

    def const(shape):
        return pl.BlockSpec(shape, lambda i, j_ref: (0,) * len(shape), pipeline_mode=pl.Buffered(1))

    return call(
        lambda *refs: second_kernel(samples, refs),
        (
            jax.ShapeDtypeStruct(pp_shape, BF16),
            jax.ShapeDtypeStruct(sec_shape, F32),
            jax.ShapeDtypeStruct(fc_shape, BF16),
            jax.ShapeDtypeStruct((2 * samples, units), F32),
        ),
        17.0,
        grid_spec=pltpu.PrefetchScalarGridSpec(
            num_scalar_prefetch=1,
            grid=(1,),
            in_specs=[const(p.shape) for p in pds] + [const(lo.shape), const(hi.shape), const(w2.shape),
                      pl.BlockSpec(memory_space=pl.ANY), const(targets.shape)],
            out_specs=(const(pp_shape), const(sec_shape), const(fc_shape), const((2 * samples, units))),
            scratch_shapes=[
                pltpu.VMEM((nxb * (ny // 2) * (nz // 2) * inner, LANES), F32),
                pltpu.VMEM((channels * samples, LANES), F32),
                pltpu.VMEM((channels, cells, units), BF16),
                pltpu.SemaphoreType.DMA((4,)),
            ],
        ),
        name="second_conv",
    )(j, *pds, lo, hi, w2, dense4, targets)


def dense_kernel(samples, own, targets_n, refs):
    (j_ref, *hp_refs, do_ref, d_ref, sec_hbm, pred_ref, bh_ref, gdo_ref, bs_ref, lo_ref, hi_ref,
     bfc, bf, dbuf, sec_ref, sems, sec_sem) = refs
    copies = dense_copies(d_ref, j_ref, dbuf, sems)
    for copy in copies:
        copy.start()
    sec_copy = pltpu.make_async_copy(sec_hbm, sec_ref, sec_sem)
    sec_copy.start()
    nxb, ny, nz, inner, _ = sec_ref.shape
    channels, cells, _ = dbuf.shape
    both = sum(ref[...] for ref in hp_refs)
    hp = both[0:samples]
    goals = both[samples:]
    hidden = leaky_relu(hp).astype(BF16).astype(F32)
    row = lax.broadcasted_iota(jnp.int32, (samples, 1), 0)
    mine = (row // own) == j_ref[0]
    lane = lax.broadcasted_iota(jnp.int32, (samples, LANES), 1)
    preds = jnp.zeros((samples, LANES), F32)
    gdo_ref[...] = jnp.zeros_like(gdo_ref)
    back = jnp.zeros_like(hp)
    for t in range(targets_n):
        weight = do_ref[t : t + 1, :]
        pred = jnp.sum(hidden * weight, axis=1, keepdims=True)
        misfit = pred - goals[:, t : t + 1]
        preds = jnp.where(lane == t, pred, preds)
        gdo_ref[t : t + 1, :] = jnp.sum(jnp.where(mine, hidden * misfit, 0.0), axis=0, keepdims=True)
        back = back + misfit * weight
    for q in range(own):
        picked = jnp.where(row == j_ref[0] * own + q, preds, 0.0)
        pred_ref[q : q + 1, :] = jnp.sum(picked, axis=0, keepdims=True)[:, :targets_n]
    bh = (back * slope_of(hp)).astype(BF16)
    bh_ref[...] = bh

    def features(t, carry):
        for u in range(8):
            ch = t * 8 + u
            out = dot_lanes(bh, dbuf[ch])
            bfc[pl.ds(pl.multiple_of(ch * samples, samples), samples), 0:cells] = out
        return carry

    size = channels // 8 // len(copies)
    for p, copy in enumerate(copies):
        copy.wait()
        lax.fori_loop(p * size, (p + 1) * size, features, 0)
    half = ny // 2
    per_half = half * (nz // 2)

    def turn(s, carry):
        turned = bfc[pl.ds(s, channels, stride=samples), 0:cells].T
        for xb in range(nxb):
            for h in range(HALVES):
                start = xb * per_half * inner + h * samples + s
                at = (xb * HALVES + h) * per_half
                bf[pl.ds(start, per_half, stride=inner), :] = turned[at : at + per_half]
        return carry

    lax.fori_loop(0, samples, turn, 0)
    count = nz // 2 * inner
    sec_copy.wait()

    def spread(t, carry):
        xb = t // half
        y3 = t % half
        start = pl.multiple_of(t * count, count)
        g = bf[pl.ds(start, count), :].reshape(nz // 2, 1, inner, LANES) * 0.125
        g = jnp.broadcast_to(g, (nz // 2, 2, inner, LANES)).reshape(nz, inner, LANES)
        for dy in range(2):
            y = 2 * y3 + dy
            slope = slope_of(sec_ref[xb, y])
            for px in range(2):
                bs_ref[2 * xb + px, y] = (g * slope[:, :, px * LANES : (px + 1) * LANES]).astype(BF16)
        return carry

    lax.fori_loop(0, nxb * half, spread, 0)
    lo_ref[...] = bs_ref[0]
    hi_ref[...] = bs_ref[2 * nxb - 1]


def dense_layers(j, hps, dense_out_t, dense4, sec, own):
    nxb, ny, nz, inner, _ = sec.shape
    channels, _, cells, units = dense4.shape
    samples = hps[0].shape[0] // 2
    targets_n = dense_out_t.shape[0]
    bs_shape = (2 * nxb, ny, nz, inner, LANES)

    def const(shape):
        return pl.BlockSpec(shape, lambda i, j_ref: (0,) * len(shape), pipeline_mode=pl.Buffered(1))

    return call(
        lambda *refs: dense_kernel(samples, own, targets_n, refs),
        (
            jax.ShapeDtypeStruct((own, targets_n), F32),
            jax.ShapeDtypeStruct((samples, units), BF16),
            jax.ShapeDtypeStruct((8, units), F32),
            jax.ShapeDtypeStruct(bs_shape, BF16),
            jax.ShapeDtypeStruct(bs_shape[1:], BF16),
            jax.ShapeDtypeStruct(bs_shape[1:], BF16),
        ),
        11.0,
        grid_spec=pltpu.PrefetchScalarGridSpec(
            num_scalar_prefetch=1,
            grid=(1,),
            in_specs=[const(hp.shape) for hp in hps]
            + [const(dense_out_t.shape)]
            + [pl.BlockSpec(memory_space=pl.ANY)] * 2,
            out_specs=(const((own, targets_n)), const((samples, units)), const((8, units)),
                       const(bs_shape), const(bs_shape[1:]), const(bs_shape[1:])),
            scratch_shapes=[
                pltpu.VMEM((channels * samples, LANES), F32),
                pltpu.VMEM((nxb * (ny // 2) * (nz // 2) * inner, LANES), F32),
                pltpu.VMEM((channels, cells, units), BF16),
                pltpu.VMEM(sec.shape, F32),
                pltpu.SemaphoreType.DMA((4,)),
                pltpu.SemaphoreType.DMA(()),
            ],
        ),
        name="dense_layers",
    )(j, *hps, dense_out_t, dense4, sec)


def collect_kernel(spaces, samples, at_bh, at_grad, r_ref, t_ref, o_ref):
    everyone = r_ref.shape[0]
    groups = everyone // spaces
    chans, _, cells, _ = o_ref.shape
    total = r_ref[0, at_grad:].astype(F32)
    for t in range(1, everyone):
        total = total + r_ref[t, at_grad:].astype(F32)
    total = total.astype(BF16)
    for t in range(everyone):
        t_ref[t] = total

    def stack(j, row):
        rows = [
            r_ref[g * spaces + j, row : row + samples].astype(F32) for g in range(groups)
        ]
        return jnp.concatenate(rows, axis=0).astype(BF16)

    b = stack(0, at_bh)
    for ch in range(chans):
        for j in range(spaces):
            o_ref[ch, j] = dot_rows(stack(j, ch * samples)[:, 0:cells], b)


def collect(received, spaces, fc_shape):
    everyone = received.shape[0]
    channels, samples, cells = fc_shape
    at_bh, at_grad, end = message_rows(everyone, fc_shape)
    return call(
        lambda *refs: collect_kernel(spaces, samples, at_bh, at_grad, *refs),
        (
            jax.ShapeDtypeStruct((everyone, end - at_grad, LANES), BF16),
            jax.ShapeDtypeStruct((channels // everyone, spaces, cells, LANES), F32),
        ),
        4.0,
        name="collect",
    )(received)


def second_grad_kernel(bs_ref, pp_ref, fc_ref, bh_ref, m_ref, acc, flat):
    planes, ny, nz, inner, _ = bs_ref.shape
    nxb = planes // 2
    half = ny // 2
    rows = 2 * nz * inner
    acc[...] = jnp.zeros_like(acc)

    def step(t, carry):
        xb = t // half
        y = 2 * (t % half)
        left = jnp.concatenate(
            [bs_ref[2 * xb + px, pl.ds(y, 2)].reshape(rows, LANES) for px in range(2)], axis=1
        ).T
        for dy in range(3):
            for dz in range(3):
                right = jnp.concatenate(
                    [
                        pp_ref[xb + kk, pl.ds(y + dy, 2), dz : dz + nz].reshape(rows, LANES)
                        for kk in range(2)
                    ],
                    axis=1,
                )
                acc[dy * 3 + dz] = acc[dy * 3 + dz] + dot(left, right)
        return carry

    lax.fori_loop(0, nxb * half, step, 0)
    mid = LANES // 2
    for o in range(9):
        both = acc[o, :LANES, 0 : 3 * mid] + acc[o, LANES:, mid : 4 * mid]
        for a in range(3):
            at = a * 9 + o
            block = at // 2 * LANES
            half_at = (at % 2) * mid
            flat[block : block + LANES, half_at : half_at + mid] = both[:, a * mid : (a + 1) * mid]
    flat[13 * LANES :, mid:] = jnp.zeros((LANES, mid), F32)
    everyone = m_ref.shape[0]
    chans = fc_ref.shape[0] // everyone
    samples, cells = fc_ref.shape[1:]
    at_bh, at_grad, _ = message_rows(everyone, fc_ref.shape)
    piece = 14 * LANES // everyone
    bh = bh_ref[...].astype(F32)
    pad = jnp.zeros((at_grad - at_bh - samples, LANES), F32)
    side = jnp.concatenate([bh, pad], axis=0).astype(BF16)
    for t in range(everyone):
        f = fc_ref[t * chans : (t + 1) * chans].astype(F32).reshape(chans * samples, cells)
        m_ref[t, 0 : chans * samples, 0:cells] = f.astype(BF16)
        m_ref[t, at_bh:at_grad] = side
        m_ref[t, at_grad : at_grad + piece] = flat[t * piece : (t + 1) * piece].astype(BF16)


def message_rows(everyone, fc_shape):
    at_bh = -(-(fc_shape[0] // everyone * fc_shape[1]) // 16) * 16
    at_grad = at_bh + -(-fc_shape[1] // 16) * 16
    return at_bh, at_grad, at_grad + 14 * LANES // everyone


def second_grad(bs, pp, fc, bh, everyone):
    rows = message_rows(everyone, fc.shape)[2]
    return call(
        second_grad_kernel,
        jax.ShapeDtypeStruct((everyone, rows, LANES), BF16),
        12.0,
        scratch_shapes=[
            pltpu.VMEM((9, 2 * LANES, 2 * LANES), F32),
            pltpu.VMEM((14 * LANES, LANES), F32),
        ],
        name="second_grad",
    )(bs, pp, fc, bh)


def second_back_kernel(bs_ref, lo_ref, hi_ref, w_ref, bp_ref, pad):
    planes, ny, nz, inner, _ = bs_ref.shape
    nxb = planes // 2
    zero = jnp.zeros((inner, LANES), BF16)
    for p in range(planes + 2):

        def fill(y, carry, p=p):
            if p == 0:
                v = lo_ref[y]
            elif p == planes + 1:
                v = hi_ref[y]
            else:
                v = bs_ref[p - 1, y]
            pad[p, y + 1, 1 : nz + 1] = v
            return carry

        lax.fori_loop(0, ny, fill, 0)
        before, after = half_pads(
            pad[p, ny, 1 : nz + 1].astype(F32), pad[p, 1, 1 : nz + 1].astype(F32)
        )
        pad[p, 0, 1 : nz + 1] = before.astype(BF16)
        pad[p, ny + 1, 1 : nz + 1] = after.astype(BF16)

        def zero_ends(y, carry, p=p):
            pad[p, y, 0] = zero
            pad[p, y, nz + 1] = zero
            return carry

        lax.fori_loop(0, ny + 2, zero_ends, 0)

    quarter = ny // 4
    rows = nz * inner
    depth = 16 * LANES

    def step(t, carry):
        xb = t // quarter
        y = 4 * (t % quarter)
        out = jnp.zeros((2 * rows, 2 * LANES), F32)
        for dz in range(3):
            pieces = []
            for jx in range(4):
                for jy in range(4):
                    pieces.append(
                        jnp.concatenate(
                            [
                                pad[2 * xb + jx, y + 2 * u + jy, dz : dz + nz].reshape(rows, LANES)
                                for u in range(2)
                            ],
                            axis=0,
                        )
                    )
            sides = []
            for px in range(2):
                blocks = [
                    w_ref[dz, jx - px].reshape(depth // 4, LANES)
                    if 0 <= jx - px <= 2
                    else jnp.zeros((depth // 4, LANES), BF16)
                    for jx in range(4)
                ]
                sides.append(jnp.concatenate(blocks, axis=0))
            out = out + dot(jnp.concatenate(pieces, axis=1), jnp.concatenate(sides, axis=1))
        out = out.astype(BF16).astype(F32) * 0.125
        mask = low_half((2 * rows, LANES))
        for px in range(2):
            v = out[:, px * LANES : (px + 1) * LANES]
            r = roll_half(v)
            for py in range(2):
                d = jnp.where(mask, v, r) if py == 0 else jnp.where(mask, r, v)
                d = d.astype(BF16).reshape(2, nz, inner, LANES)
                for u in range(2):
                    bp_ref[2 * xb + px, y + 2 * u + py] = d[u]
        return carry

    lax.fori_loop(0, nxb * quarter, step, 0)


def second_back(bs, lo, hi, w3):
    planes, ny, nz, inner, _ = bs.shape
    return call(
        second_back_kernel,
        jax.ShapeDtypeStruct(bs.shape, BF16),
        12.0,
        scratch_shapes=[pltpu.VMEM((planes + 2, ny + 2, nz + 2, inner, LANES), BF16)],
        name="second_back",
    )(bs, lo, hi, w3)


def sums_kernel(local_count, total_count, count, refs):
    f_ref, bp_ref, gs_ref, *st_refs = refs[: count + 3]
    o_ref, act_ref, acc = refs[count + 3 :]
    i = pl.program_id(0)
    mean, inverse = group_stats(st_refs, local_count, total_count)
    scale = wide(gs_ref[0:1] * inverse)
    mean, shift = wide(mean), wide(gs_ref[1:2])
    nz, inner = f_ref.shape[2:4]

    @pl.when(i == 0)
    def _():
        acc[...] = jnp.zeros_like(acc)

    size = 4

    def step(yb, carry):
        cross = acc[0]
        plain = acc[1]
        for z in range(0, nz, size):
            dev = f_ref[0, yb, z : z + size].reshape(size * inner, 2 * LANES) - mean
            slope = slope_of(dev * scale + shift)
            g = bp_ref[0, yb, z // 2 : (z + size) // 2].astype(F32)
            g = jnp.broadcast_to(g.reshape(size // 2, 1, inner, LANES), (size // 2, 2, inner, LANES))
            g = g.reshape(size * inner, LANES)
            active = slope * jnp.concatenate([g, g], axis=1)
            cross = cross + jnp.sum((active * dev).reshape(-1, 8, 2 * LANES), axis=0)
            plain = plain + jnp.sum(active.reshape(-1, 8, 2 * LANES), axis=0)
            act_ref[0, yb, z : z + size] = active.reshape(size, inner, 2 * LANES)
        acc[0] = cross
        acc[1] = plain
        return carry

    lax.fori_loop(0, f_ref.shape[1], step, 0)

    @pl.when(i == pl.num_programs(0) - 1)
    def _():
        rows = [jnp.sum(acc[k], axis=0, keepdims=True) for k in range(2)]
        rows = [both_halves(r[:, :LANES] + r[:, LANES:]) for r in rows]
        o_ref[...] = jnp.concatenate([rows[0] * inverse, rows[1]], axis=0)


def norm_sums(f, bp, stats, gs, local_count, total_count):
    return call(
        lambda *refs: sums_kernel(local_count, total_count, len(stats), refs),
        (jax.ShapeDtypeStruct((2, LANES), F32), jax.ShapeDtypeStruct(f.shape, F32)),
        13.0,
        grid=(f.shape[0],),
        in_specs=[
            pl.BlockSpec((1,) + f.shape[1:], lambda i: (i, 0, 0, 0, 0)),
            pl.BlockSpec((1,) + bp.shape[1:], lambda i: (i, 0, 0, 0, 0)),
            whole_spec(gs.shape),
        ] + [whole_spec(st.shape) for st in stats],
        out_specs=(
            whole_spec((2, LANES)),
            pl.BlockSpec((1,) + f.shape[1:], lambda i: (i, 0, 0, 0, 0)),
        ),
        scratch_shapes=[pltpu.VMEM((2, 8, 2 * LANES), F32)],
        name="norm_sums",
    )(f, bp, gs, *stats)


def first_grad_kernel(local_count, total_count, c, count, refs):
    f_ref, act_ref, xa_ref, xc_ref, xe_ref, gs_ref, gdo_ref = refs[:7]
    st_refs = refs[7 : 7 + count]
    sum_refs = refs[7 + count : 7 + 2 * count]
    g_ref, acc, cur, left_a, left_b = refs[7 + 2 * count :]
    i = pl.program_id(0)
    end = pl.num_programs(0) - 1
    mean, inverse = group_stats(st_refs, local_count, total_count)
    group_sums = sum(ref[...] for ref in sum_refs) * (1.0 / total_count)
    scale = gs_ref[0:1] * inverse
    cross = wide(scale * inverse * group_sums[0:1])
    plain = wide(scale * group_sums[1:2])
    scale, mean = wide(scale), wide(mean)
    nz = f_ref.shape[2]
    inner = f_ref.shape[3]
    rows = nz * inner

    @pl.when(i == 0)
    def _():
        acc[...] = jnp.zeros_like(acc)

    def load(k, ref, at):
        def body(m, carry):
            cur[k, m] = ref[at, m]
            return carry

        lax.fori_loop(0, cur.shape[1], body, 0)

    pl.when(i == 0)(lambda: load(0, xe_ref, 0))
    pl.when(i > 0)(lambda: load(0, xa_ref, 0))
    pl.when(i == end)(lambda: load(1, xe_ref, 1))
    pl.when(i < end)(lambda: load(1, xc_ref, 0))

    def left(yb, ref):
        dev = f_ref[0, yb].reshape(rows, 2 * LANES) - mean
        active = act_ref[0, yb].reshape(rows, 2 * LANES)
        ref[...] = (active * scale - (dev * cross + plain)).astype(BF16).T

    def add(yb, ref):
        for dz in range(3):
            for kk in range(2):
                right = jnp.concatenate(
                    [cur[kk, yb + mm, dz : dz + nz].reshape(rows, LANES) for mm in range(2)],
                    axis=1,
                )
                acc[dz * 2 + kk] = acc[dz * 2 + kk] + dot(ref[...], right)

    blocks = f_ref.shape[1]

    def step(t, carry):
        left(2 * t + 1, left_b)
        add(2 * t, left_a)
        left(jnp.minimum(2 * t + 2, blocks - 1), left_a)
        add(2 * t + 1, left_b)
        return carry

    left(0, left_a)
    lax.fori_loop(0, blocks // 2, step, 0)

    @pl.when(i == end)
    def _():
        co = LANES // 2
        blocks = -(-27 * c // LANES)
        g_ref[(blocks - 1) * co :, :] = jnp.zeros((g_ref.shape[0] - (blocks - 1) * co, LANES), F32)
        g_ref[blocks * co : blocks * co + 2, :] = sum_refs[0][...]
        g_ref[blocks * co + 8 : blocks * co + 16, :] = gdo_ref[...]
        for a in range(3):
            for b in range(3):
                for d in range(3):
                    total = None
                    for px in range(2):
                        for py in range(2):
                            xw, yw = a + px, b + py
                            at = (yw // 2) * LANES + (yw % 2) * 2 * c + (xw % 2) * c
                            top = (px * 2 + py) * co
                            part = acc[d * 2 + xw // 2, top : top + co, at : at + c]
                            total = part if total is None else total + part
                    at = offset(a, b, d) * c
                    row = at // LANES * co
                    g_ref[row : row + co, at % LANES : at % LANES + c] = total


def first_grad(f, active, xi, xe, gs, gdo, stats, sums, c, local_count, total_count, rows):
    x_block = (1,) + xi.shape[1:]
    out = (rows, LANES)
    return call(
        lambda *refs: first_grad_kernel(local_count, total_count, c, len(stats), refs),
        jax.ShapeDtypeStruct(out, F32),
        30.0,
        grid=(f.shape[0],),
        in_specs=[
            pl.BlockSpec((1,) + f.shape[1:], lambda i: (i, 0, 0, 0, 0)),
            pl.BlockSpec((1,) + f.shape[1:], lambda i: (i, 0, 0, 0, 0)),
            pl.BlockSpec(x_block, lambda i: (i, 0, 0, 0, 0)),
            pl.BlockSpec(x_block, lambda i: (i + 1, 0, 0, 0, 0)),
        ] + [whole_spec(a.shape) for a in (xe, gs, gdo, *stats, *sums)],
        out_specs=whole_spec(out),
        scratch_shapes=[
            pltpu.VMEM((6, 2 * LANES, 2 * LANES), F32),
            pltpu.VMEM(xe.shape, BF16),
            pltpu.VMEM((2 * LANES, f.shape[2] * f.shape[3]), BF16),
            pltpu.VMEM((2 * LANES, f.shape[2] * f.shape[3]), BF16),
        ],
        name="first_grad",
    )(f, active, xi, xi, xe, gs, gdo, *stats, *sums)


def add_kernel(r_ref, o_ref):
    total = r_ref[0]
    for t in range(1, r_ref.shape[0]):
        total = total + r_ref[t]
    total = total.astype(BF16)
    for t in range(o_ref.shape[0]):
        o_ref[t] = total


def add_parts(parts):
    return call(add_kernel, jax.ShapeDtypeStruct(parts.shape, BF16), 2.0, name="add_parts")(parts)


def gather_all(value, axis):
    count = lax.axis_size(axis)
    others = [
        lax.ppermute(value, axis, [(i, (i + k) % count) for i in range(count)])
        for k in range(1, count)
    ]
    return [value] + others


def swap(parts, axes):
    return lax.all_to_all(parts, axes, split_axis=0, concat_axis=0, tiled=True)


def finish_second_kernel(r_ref, g_ref):
    columns = g_ref.shape[0]
    for k in range(r_ref.shape[0]):
        width = min(LANES, columns - k * LANES)
        g_ref[k * LANES : k * LANES + width, :] = r_ref[k].astype(F32).T[0:width]


def finish_first_kernel(r_ref, g_ref, n_ref, gdo_ref):
    co, columns = g_ref.shape
    blocks = -(-columns // LANES)
    for k in range(blocks):
        width = min(LANES, columns - k * LANES)
        g_ref[:, k * LANES : k * LANES + width] = r_ref[k * co : (k + 1) * co].astype(F32)[:, 0:width]
    tail = r_ref[blocks * co : blocks * co + 16].astype(F32)
    n_ref[...] = tail[0:2, 0 : n_ref.shape[1]]
    gdo_ref[...] = tail[8 : 8 + gdo_ref.shape[0]]


def swap_edges(first, last, axis):
    count = lax.axis_size(axis)
    before = lax.ppermute(last, axis, [(i, i + 1) for i in range(count - 1)])
    after = lax.ppermute(first, axis, [(i + 1, i) for i in range(count - 1)])
    return before, after


def shards(inputs, conv_in, norm_gain, norm_shift, conv_out, dense_in, dense_out, targets):
    samples, c, planes, cells = inputs.shape
    spaces = lax.axis_size("space")
    groups = lax.axis_size("dp")
    units = dense_in.shape[1]
    channels = conv_out.shape[0]
    own = targets.shape[0]
    local_count = float(samples * planes * cells)
    total_count = local_count * spaces

    everyone = groups * spaces
    world = ("dp", "space")

    x = inputs.reshape(samples, c * planes, cells)
    first, last = edge_planes(x, planes, c)
    before, after = swap_edges(first, last, "space")
    w1 = first_weights(conv_in)
    xi = prepare(x, planes, c)
    gs = jnp.stack([norm_gain, norm_shift])
    gs = jnp.concatenate([gs, gs], axis=1)
    j = lax.axis_index("space").astype(jnp.int32).reshape(1)
    dense4 = dense_in.reshape(channels, spaces, dense_in.shape[0] // (channels * spaces), units)

    f, xe, st = first_conv(xi, before, after, w1, planes)
    stats = gather_all(st, "space")
    w2, v3 = second_weights(conv_out)
    outer, edge_lo, edge_hi = normalise_pool(f, stats, gs, local_count, total_count, True)
    lo, hi = swap_edges(edge_lo, edge_hi, "space")
    pds = [outer]
    if planes > 4:
        pds += normalise_pool(f, stats, gs, local_count, total_count, False)
    pp, sec, fc, partial = second_conv(j, pds, lo, hi, w2, dense4, targets, samples)
    hps = gather_all(partial, "space")
    predictions, bh, gdo, bs, bs_first, bs_last = dense_layers(
        j, hps, dense_out.astype(F32).T, dense4, sec, own
    )
    bs_lo, bs_hi = swap_edges(bs_first, bs_last, "space")
    message = second_grad(bs, pp, fc, bh, everyone)
    received = swap(message, world)
    bp = second_back(bs, bs_lo, bs_hi, v3)
    own_sums, active = norm_sums(f, bp, stats, gs, local_count, total_count)
    sums = gather_all(own_sums, "space")
    totals, grad_dense_in = collect(received, spaces, fc.shape)
    totals = swap(totals, world)
    used = -(-conv_in.shape[1] // LANES) * conv_in.shape[0] + 16
    rows = -(-used // everyone)
    rows = (-(-rows // 8) * 8 if rows > 8 else rows) * everyone
    local_in = first_grad(
        f, active, xi, xe, gs, gdo, stats, sums, c, local_count, total_count, rows
    )
    parts = swap(local_in.reshape(everyone, -1, LANES), world)
    grad_conv_out = call(
        finish_second_kernel,
        jax.ShapeDtypeStruct(conv_out.shape[::-1], F32),
        2.0,
        name="finish_second",
    )(totals.reshape(14, LANES, LANES))
    sent = add_parts(parts)
    totals = swap(sent, world)
    grad_conv_in, grad_norm, grad_dense_out = call(
        finish_first_kernel,
        (
            jax.ShapeDtypeStruct(conv_in.shape, F32),
            jax.ShapeDtypeStruct((2, norm_gain.shape[0]), F32),
            jax.ShapeDtypeStruct(dense_out.shape[::-1], F32),
        ),
        name="finish_first",
    )(totals.reshape(rows, LANES))
    return (
        grad_conv_in,
        grad_norm,
        grad_conv_out.T,
        grad_dense_in.reshape(-1, units),
        grad_dense_out.T,
        predictions,
    )


def solution(mesh):
    placed = (P("dp", None, "space", None), P(), P(), P(), P(), P(), P(), P(("dp", "space"), None))
    return jax.shard_map(
        shards,
        mesh=mesh,
        in_specs=placed,
        out_specs=(P(), P(), P(), P(("dp", "space"), None), P(), P(("dp", "space"), None)),
        check_vma=False,
    )
```
